32 devices in a mesh: space: 8 (over z, y), mem: 4 (over x, core).
Axes of the slice: x: 2, y: 2, z: 4, core: 2. Of those that a mesh axis runs over, the one named last changes fastest.
Arguments:
- prior_ensemble: float32 [512, 32, 128], P('mem', 'space'), may hold values from -70 to 70
- stencil_factors: float32 [4, 32, 128], P(None, 'space'), may hold values from 0.02 to 0.22
- sea_mask: int32 [32, 128], P('space'), may hold values 0 or 1
- measured_site_positions: int32 [8, 128], P('space'), may hold values from 0 to 511
- measured_data: float32 [1024], P('space'), may hold values from -16 to 16
- measurement_precision: float32 [1024], P('space'), may hold values from 0.5 to 2
- cotangent: float32 [512, 32, 128], P('mem', 'space'), may hold values from -6 to 6
Outputs:
- grad_prior: float32 [512, 32, 128], P('mem', 'space')
- grad_coef: float32 [4, 32, 128], P(None, 'space')
The draws below stay inside these ranges and needn't reach their ends.
Inputs may be any that keep to these rules, and one draw needn't show every extreme that they name: `measured_site_positions`: the flat position row * 128 + column, within its strip of 4 rows, of each observed cell; strip s holds rows s * 4 to (s + 1) * 4 - 1. `sea_mask`: 1 marks a sea cell, 0 a land cell.
All inputs are finite; a program needn't handle non-finite values. No bound on the sum of `sea_mask` on one device may be relied on, other than what follows from the above.
Results may differ from the reference program's by a relative error of at most 0.0003.
Values sent between devices are 32-bit elements; how exact they have to be, the bound alone decides.
A program may use at most 64 MiB of HBM per device.

```python
import math
import jax
import jax.numpy as jnp
from jax import lax

SAMPLE_TOTAL = 512
MESH_LONGITUDES = 128
BAND_LATITUDES = 4
K = 128
ITERS = 2
TILES = 8
MESH_LATITUDES = 32
NOBS = 1024


def draw_prior_ensemble(key, part):
    key_scale, key_noise = jax.random.split(key, 2)
    member_pos = (jnp.arange(SAMPLE_TOTAL, dtype=jnp.float32) + jax.random.uniform(key_scale, (SAMPLE_TOTAL,))) / SAMPLE_TOTAL
    row_pos = jnp.arange(MESH_LATITUDES, dtype=jnp.float32) / MESH_LATITUDES
    scales = 0.3 * 10.0 ** member_pos
    strip_ramp = 3.0 ** row_pos
    noise_field = jax.random.truncated_normal(key_noise, -4.0, 4.0, (SAMPLE_TOTAL, MESH_LATITUDES, MESH_LONGITUDES))
    return (scales[:, None, None] * strip_ramp[None, :, None] * noise_field).astype(jnp.float32)


def with_ends(result, stream_key, least, largest):
    longest = result.shape.index(max(result.shape))
    spots = []
    for shift in (0, 1):
        where = [jax.random.randint(jax.random.fold_in(stream_key, axis), (), 0, length) for axis, length in enumerate(result.shape)]
        where[longest] = (where[longest] + shift) % result.shape[longest]
        spots.append(tuple(where))
    return result.at[spots[0]].set(least).at[spots[1]].set(largest)


def block_levels(own_key, dims, cuts, low, high):
    def one(dim, blocks):
        draws = jax.random.uniform(jax.random.fold_in(jax.random.fold_in(own_key, 6), dim), (blocks,), jnp.float32, low / len(cuts), high / len(cuts))
        return jnp.repeat(jnp.exp(draws), dims[dim] // blocks).reshape((-1,) + (1,) * (len(dims) - dim - 1))

    loudness = one(*cuts[0])
    for cut in cuts[1:]:
        loudness = loudness * one(*cut)
    return loudness


def normal_values(own_key, shape, width, most, pieces=(), kind=jnp.bfloat16):
    gain = block_levels(own_key, shape, pieces, -0.22, 0.18) if pieces else 1.0
    drawn = jax.random.normal(own_key, shape, jnp.float32) * width * gain
    return jnp.minimum(jnp.maximum(drawn, -most), most).astype(kind)


def setup_inputs(seed: int = 0) -> dict:
    splits = jax.random.split(jax.random.key(seed), 8)
    return {
        "prior_ensemble": draw_prior_ensemble(jax.random.fold_in(splits[7], 71), 0),
        "stencil_factors": jnp.clip(0.02 + 0.2 * jax.random.uniform(splits[1], (4, MESH_LATITUDES, MESH_LONGITUDES), jnp.float32) ** block_levels(splits[1], (4, MESH_LATITUDES, MESH_LONGITUDES), ((1, 8),), -0.2, 0.2), 0.02, 0.22),
        "sea_mask": with_ends((jax.random.randint(splits[2], (MESH_LATITUDES, MESH_LONGITUDES), 0, 5) < 4).astype(jnp.int32), jax.random.fold_in(splits[2], 1), 0, 1),
        "measured_site_positions": with_ends(jax.random.randint(splits[3], (TILES, K), 0, BAND_LATITUDES * MESH_LONGITUDES), jax.random.fold_in(splits[3], 1), 0, (BAND_LATITUDES * MESH_LONGITUDES) - 1).astype(jnp.int32),
        "measured_data": normal_values(splits[4], (NOBS,), 4.0, 16.0, ((0, 8),), jnp.float32),
        "measurement_precision": jnp.clip(jnp.exp(math.log(2.0) - 1.3862944 * jax.random.uniform(splits[5], (NOBS,), jnp.float32) ** block_levels(splits[5], (NOBS,), ((0, 8),), -0.2, 0.2)), 0.5, 2.0),
        "cotangent": normal_values(splits[6], (SAMPLE_TOTAL, MESH_LATITUDES, MESH_LONGITUDES), 1.0, 6.0, ((0, 4), (1, 8)), jnp.float32),
    }


highest = lax.Precision.HIGHEST

def product(left_side, right_side):
    return jnp.dot(left_side, right_side, precision=highest, preferred_element_type=jnp.float32)

def substep(state_band_piece, stencil_factors, ocean_share):
    padded = jnp.pad(state_band_piece, ((0, 0), (1, 1), (1, 1)))
    northern = padded[:, :-2, 1:-1]
    southern = padded[:, 2:, 1:-1]
    western = padded[:, 1:-1, :-2]
    eastern = padded[:, 1:-1, 2:]
    advanced = state_band_piece + stencil_factors[0] * (northern - state_band_piece) + stencil_factors[1] * (southern - state_band_piece) + stencil_factors[2] * (western - state_band_piece) + stencil_factors[3] * (eastern - state_band_piece)
    return ocean_share * advanced

def predicted_samples(state_band_piece, stencil_factors, ocean_share):
    return substep(substep(state_band_piece, stencil_factors, ocean_share), stencil_factors, ocean_share)

def corrected_state(predict_advance, measured_site_positions, measured_data, measurement_precision):
    covariance_factor_matrix = jnp.sqrt(jnp.float32(SAMPLE_TOTAL - 1))
    sample_average = lax.optimization_barrier(jnp.mean(predict_advance, axis=0))
    sample_deviations = (predict_advance - sample_average) / covariance_factor_matrix
    mesh_bands = predict_advance.reshape(SAMPLE_TOTAL, MESH_LATITUDES // BAND_LATITUDES, BAND_LATITUDES * MESH_LONGITUDES)
    where_seen = jnp.broadcast_to(measured_site_positions[None, :, :], (SAMPLE_TOTAL, MESH_LATITUDES // BAND_LATITUDES, K))
    picked = jnp.take_along_axis(mesh_bands, where_seen, axis=2).reshape(SAMPLE_TOTAL, NOBS)
    observed = picked + 0.5 * jnp.tanh(picked)
    observed_mean = lax.optimization_barrier(jnp.mean(observed, axis=0))
    obs_anom = (observed - observed_mean) * measurement_precision / covariance_factor_matrix
    innovation = measurement_precision * (measured_data - observed_mean)
    identity = jnp.eye(SAMPLE_TOTAL, dtype=jnp.float32)
    system = identity + product(obs_anom, obs_anom.T)
    norm_scale = jnp.sqrt(jnp.sum(system * system))
    obs_pull = product(obs_anom, innovation)
    approach = system / norm_scale
    polar = identity
    for iteration in range(ITERS):
        factor = 1.5 * identity - 0.5 * product(polar, approach)
        approach = product(approach, factor)
        polar = product(factor, polar)
    transform = polar / jnp.sqrt(norm_scale)
    mean_weights = product(transform, product(transform, obs_pull))
    mixing = covariance_factor_matrix * transform + mean_weights[None, :]
    flattened = sample_deviations.reshape(SAMPLE_TOTAL, MESH_LATITUDES * MESH_LONGITUDES)
    return sample_average + product(mixing, flattened).reshape(SAMPLE_TOTAL, MESH_LATITUDES, MESH_LONGITUDES)

def reference(prior_ensemble, stencil_factors, sea_mask, measured_site_positions, measured_data, measurement_precision, cotangent):
    ocean_share = sea_mask.astype(jnp.float32)
    gathered_samples = prior_ensemble.reshape(SAMPLE_TOTAL // 64, 64, MESH_LATITUDES, MESH_LONGITUDES)
    predict_advance = lax.map(lambda sample_band_piece: predicted_samples(sample_band_piece, stencil_factors, ocean_share), gathered_samples).reshape(SAMPLE_TOTAL, MESH_LATITUDES, MESH_LONGITUDES)
    advance_product, cotangent_mapping = jax.vjp(lambda state_argument: corrected_state(state_argument, measured_site_positions, measured_data, measurement_precision), predict_advance)
    field_bar, = cotangent_mapping(cotangent)

    def block_grad(block_pair):
        sample_band_piece, block_bar = block_pair
        overall_answer, reverse_sweep = jax.vjp(lambda state_argument, stencil_argument: predicted_samples(state_argument, stencil_argument, ocean_share), sample_band_piece, stencil_factors)
        return reverse_sweep(block_bar)
    prior_bar, coef_parts = lax.map(block_grad, (gathered_samples, field_bar.reshape(SAMPLE_TOTAL // 64, 64, MESH_LATITUDES, MESH_LONGITUDES)))
    return (prior_bar.reshape(SAMPLE_TOTAL, MESH_LATITUDES, MESH_LONGITUDES), lax.optimization_barrier(jnp.sum(coef_parts, axis=0)) / jnp.sqrt(jnp.float32(SAMPLE_TOTAL)))
```

```python
import functools
import jax
import jax.numpy as jnp
from jax import lax
from jax.experimental import pallas as pl
from jax.experimental.pallas import tpu as pltpu
from jax.sharding import PartitionSpec as P

MESH = pl.DeviceIdType.MESH
HIGH = lax.Precision.HIGH
HIGHEST = lax.Precision.HIGHEST
VMEM_SPEC = pl.BlockSpec(memory_space=pltpu.VMEM)


def dot(a, b, a_dims, b_dims, precision=HIGH):
    return lax.dot_general(
        a, b, ((a_dims, b_dims), ((), ())), precision=precision, preferred_element_type=jnp.float32
    )


def mm(a, b):
    return dot(a, b, (1,), (0,))


def remote(src, dst, send, recv, s, m):
    return pltpu.make_async_remote_copy(
        src_ref=src, dst_ref=dst, send_sem=send, recv_sem=recv, device_id=(s, m), device_id_type=MESH
    )


def params(ident):
    return pltpu.CompilerParams(collective_id=ident, has_side_effects=True)


def halo_body(n_space, last, first, low, high, send, recv):
    s, m = lax.axis_index("space"), lax.axis_index("mem")
    barrier = pltpu.get_barrier_semaphore()
    has_low, has_high = s > 0, s < n_space - 1

    @pl.when(has_low)
    def _():
        pl.semaphore_signal(barrier, inc=1, device_id=(s - 1, m), device_id_type=MESH)

    @pl.when(has_high)
    def _():
        pl.semaphore_signal(barrier, inc=1, device_id=(s + 1, m), device_id_type=MESH)

    pl.semaphore_wait(barrier, has_low.astype(jnp.int32) + has_high.astype(jnp.int32))

    up = remote(last, low, send.at[0], recv.at[0], s + 1, m)
    down = remote(first, high, send.at[1], recv.at[1], s - 1, m)

    @pl.when(has_high)
    def _():
        up.start()

    @pl.when(has_low)
    def _():
        down.start()

    def finish():
        @pl.when(has_low)
        def _():
            up.wait_recv()
            down.wait_send()

        @pl.when(has_high)
        def _():
            down.wait_recv()
            up.wait_send()

    return finish


def halo(n_space, last, first, ident):
    def body(last_ref, first_ref, low, high, send, recv):
        halo_body(n_space, last_ref, first_ref, low, high, send, recv)()

    shape = jax.ShapeDtypeStruct(last.shape, last.dtype)
    low, high = pl.pallas_call(
        body,
        out_shape=(shape, shape),
        in_specs=[VMEM_SPEC] * 2,
        out_specs=(VMEM_SPEC,) * 2,
        scratch_shapes=[pltpu.SemaphoreType.DMA((2,)), pltpu.SemaphoreType.DMA((2,))],
        compiler_params=params(ident),
        name="halo",
    )(last, first)
    s = lax.axis_index("space")
    return jnp.where(s > 0, low, 0.0), jnp.where(s < n_space - 1, high, 0.0)


def gather_members(n_mem, arrays, dims, ident):
    count = len(arrays)

    def body(*refs):
        ins, outs = refs[:count], refs[count : 2 * count]
        send, recv, own = refs[2 * count :]
        s, m = lax.axis_index("space"), lax.axis_index("mem")
        barrier = pltpu.get_barrier_semaphore()
        for k in range(1, n_mem):
            pl.semaphore_signal(
                barrier, inc=1, device_id=(s, lax.rem(m + k, n_mem)), device_id_type=MESH
            )

        def part(i, which):
            width = arrays[i].shape[dims[i]]
            where = [slice(None)] * arrays[i].ndim
            where[dims[i]] = pl.ds(pl.multiple_of(which * width, width), width)
            return outs[i].at[tuple(where)]

        mine = [pltpu.make_async_copy(ins[i], part(i, m), own.at[i]) for i in range(count)]
        for copy in mine:
            copy.start()
        pl.semaphore_wait(barrier, n_mem - 1)
        copies = []
        for k in range(1, n_mem):
            for i in range(count):
                copy = remote(
                    ins[i], part(i, m), send.at[i, k], recv.at[i, k], s, lax.rem(m + k, n_mem)
                )
                copy.start()
                copies.append(copy)
        for copy in copies:
            copy.wait()
        for copy in mine:
            copy.wait()

    shapes = []
    for array, dim in zip(arrays, dims):
        shape = list(array.shape)
        shape[dim] *= n_mem
        shapes.append(jax.ShapeDtypeStruct(tuple(shape), array.dtype))
    return pl.pallas_call(
        body,
        out_shape=tuple(shapes),
        in_specs=[VMEM_SPEC] * count,
        out_specs=(VMEM_SPEC,) * count,
        scratch_shapes=[
            pltpu.SemaphoreType.DMA((count, n_mem)),
            pltpu.SemaphoreType.DMA((count, n_mem)),
            pltpu.SemaphoreType.DMA((count,)),
        ],
        compiler_params=params(ident),
        name="gather_members",
    )(*arrays)


def reduce_gather(n_space, n_mem, rows, ident):
    pieces, height, width = rows.shape
    near = 2 if n_space % 2 == 0 else 1
    far = n_space // near
    half = 2 if n_mem % 2 == 0 else 1
    wide = n_mem // half
    group = max(1, far // 4)
    groups = far // group

    def body(x, out, buf, rs_send, rs_recv, own, a_send, a_recv, b_send, b_recv, p_send, p_recv, q_send, q_recv):
        s, m = lax.axis_index("space"), lax.axis_index("mem")
        a, b = s // near, lax.rem(s, near)
        p, q = m // half, lax.rem(m, half)
        barrier = pltpu.get_barrier_semaphore()
        peers = [(lax.rem(s + k, n_space), m) for k in range(1, n_space)]
        peers += [(s, lax.rem(p + k, wide) * half + q) for k in range(1, wide)]
        peers += [(s, p * half + lax.rem(q + k, half)) for k in range(1, half)]
        for peer in peers:
            pl.semaphore_signal(barrier, inc=1, device_id=peer, device_id_type=MESH)
        mine = pltpu.make_async_copy(x.at[s], buf.at[s], own.at[0])
        mine.start()
        pl.semaphore_wait(barrier, len(peers))
        scatter = []
        for k in range(1, n_space):
            to = lax.rem(s + k, n_space)
            copy = remote(x.at[to], buf.at[s], rs_send.at[k], rs_recv.at[k], to, m)
            copy.start()
            scatter.append(copy)
        mine.wait()
        for copy in scatter:
            copy.wait_recv()
        total = buf[0]
        for k in range(1, n_space):
            total = total + buf[k]
        out[m, b, a] = total

        waits = list(scatter)
        stage_a = []
        for k in range(1, far):
            to = lax.rem(a + k, far)
            copy = remote(
                out.at[m, b, a], out.at[m, b, a], a_send.at[k], a_recv.at[k], to * near + b, m
            )
            copy.start()
            stage_a.append(copy)
        if group == 1:
            a_steps = [([], a)] + [([stage_a[k - 1]], lax.rem(a + far - k, far)) for k in range(1, far)]
        else:
            a_steps = [(stage_a if g == 0 else [], g * group) for g in range(groups)]
        steps_b = []
        for index, (needs, start) in enumerate(a_steps):
            for copy in needs:
                copy.wait_recv()
            steps_b.append((start, index))
            flow(
                out, s, m, b, p, q, start, index, 0, group, near, half, wide,
                b_send, b_recv, p_send, p_recv, q_send, q_recv, waits,
            )
        waits += stage_a
        for start, index in steps_b:
            pend = []
            for kb in range(1, near):
                pend.append((start, index, kb))
            for start_, index_, kb in pend:
                from_b = lax.rem(b + near - kb, near)
                piece = out.at[m, from_b, pl.ds(start_, group)]
                remote(piece, piece, b_send.at[kb, index_], b_recv.at[kb, index_], s, m).wait_recv()
                flow(
                    out, s, m, from_b, p, q, start_, index_, kb, group, near, half, wide,
                    None, None, p_send, p_recv, q_send, q_recv, waits,
                )
        for start, index in steps_b:
            for kb in range(near):
                which_b = lax.rem(b + near - kb, near)
                for kp in range(1, wide):
                    from_p = lax.rem(p + wide - kp, wide)
                    piece = out.at[from_p * half + q, which_b, pl.ds(start, group)]
                    remote(
                        piece, piece, p_send.at[kp, kb, index], p_recv.at[kp, kb, index], s, m
                    ).wait_recv()
                    for kq in range(1, half):
                        to_q = lax.rem(q + kq, half)
                        copy = remote(
                            piece, piece, q_send.at[kq, kp, kb, index], q_recv.at[kq, kp, kb, index],
                            s, p * half + to_q,
                        )
                        copy.start()
                        waits.append(copy)
        for start, index in steps_b:
            for kb in range(near):
                which_b = lax.rem(b + near - kb, near)
                for kp in range(wide):
                    from_p = lax.rem(p + wide - kp, wide)
                    for kq in range(1, half):
                        from_q = lax.rem(q + half - kq, half)
                        piece = out.at[from_p * half + from_q, which_b, pl.ds(start, group)]
                        remote(
                            piece, piece, q_send.at[kq, kp, kb, index],
                            q_recv.at[kq, kp, kb, index], s, m,
                        ).wait_recv()
        for copy in waits:
            copy.wait_send()

    def flow(
        out, s, m, which_b, p, q, start, index, kb, group, near, half, wide,
        b_send, b_recv, p_send, p_recv, q_send, q_recv, waits,
    ):
        piece = out.at[m, which_b, pl.ds(start, group)]
        for kp in range(1, wide):
            copy = remote(
                piece, piece, p_send.at[kp, kb, index], p_recv.at[kp, kb, index],
                s, lax.rem(p + kp, wide) * half + q,
            )
            copy.start()
            waits.append(copy)
        if b_send is not None:
            for k in range(1, near):
                to = (s // near) * near + lax.rem(which_b + k, near)
                copy = remote(piece, piece, b_send.at[k, index], b_recv.at[k, index], to, m)
                copy.start()
                waits.append(copy)
        for kq in range(1, half):
            copy = remote(
                piece, piece, q_send.at[kq, 0, kb, index], q_recv.at[kq, 0, kb, index],
                s, p * half + lax.rem(q + kq, half),
            )
            copy.start()
            waits.append(copy)

    dma = pltpu.SemaphoreType.DMA
    out = pl.pallas_call(
        body,
        out_shape=jax.ShapeDtypeStruct((n_mem, near, far, height, width), rows.dtype),
        in_specs=[VMEM_SPEC],
        out_specs=VMEM_SPEC,
        scratch_shapes=[
            pltpu.VMEM(rows.shape, rows.dtype),
            dma((n_space,)), dma((n_space,)), dma((1,)),
            dma((far,)), dma((far,)),
            dma((near, groups)), dma((near, groups)),
            dma((wide, near, groups)), dma((wide, near, groups)),
            dma((half, wide, near, groups)), dma((half, wide, near, groups)),
        ],
        compiler_params=params(ident),
        name="reduce_gather",
    )(rows)
    return out


def neighbours(ext):
    center, north, south = ext[1:-1], ext[:-2], ext[2:]
    border = jnp.zeros_like(center[..., :1])
    west = jnp.concatenate([border, center[..., :-1]], axis=-1)
    east = jnp.concatenate([center[..., 1:], border], axis=-1)
    return center, north, south, west, east


def substep(ext, coef, sea):
    center, north, south, west, east = neighbours(ext)
    return sea * (
        center
        + coef[0] * (north - center)
        + coef[1] * (south - center)
        + coef[2] * (west - center)
        + coef[3] * (east - center)
    )


def transpose_step(ext, coef_ext):
    center = ext[1:-1]
    inner = coef_ext[:, 1:-1]
    from_south = coef_ext[0, 2:] * ext[2:]
    from_north = coef_ext[1, :-2] * ext[:-2]
    border = jnp.zeros_like(center[..., :1])
    from_east = jnp.concatenate([(inner[2] * center)[..., 1:], border], axis=-1)
    from_west = jnp.concatenate([border, (inner[3] * center)[..., :-1]], axis=-1)
    keeping = 1.0 - inner[0] - inner[1] - inner[2] - inner[3]
    return center * keeping + from_south + from_north + from_east + from_west


def coef_terms(weight, ext):
    center, north, south, west, east = neighbours(ext)
    return jnp.stack(
        [jnp.sum(weight * (side - center), axis=1) for side in (north, south, west, east)]
    )


def local(n_space, n_mem, prior, stencil, sea_mask, sites, data, precision, cotangent):
    members, rows, cols = prior.shape
    total = members * n_mem
    scale = jnp.sqrt(jnp.float32(total - 1))
    m = lax.axis_index("mem")
    prior_t = jnp.transpose(prior, (1, 0, 2))
    cot_t = jnp.transpose(cotangent, (1, 0, 2))
    aux = jnp.concatenate(
        [
            jnp.transpose(stencil, (1, 0, 2)),
            sea_mask.astype(jnp.float32)[:, None],
            jnp.zeros((rows, 3, cols), jnp.float32),
        ],
        axis=1,
    )
    packed = jnp.concatenate([prior_t, aux], axis=1)
    low, high = halo(n_space, packed[-2:], packed[:2], 1)
    (cot_full,) = gather_members(n_mem, [cot_t], [1], 2)
    ext = jnp.concatenate([low, packed, high], axis=0)
    prior_ext = ext[:, :members]
    coef_ext = jnp.transpose(ext[:, members : members + 4], (1, 0, 2))[:, :, None]
    sea_ext = ext[:, members + 4][:, None]
    first_ext = substep(prior_ext, coef_ext[:, 1:-1], sea_ext[1:-1])
    state = substep(first_ext, coef_ext[:, 2:-2], sea_ext[2:-2])
    cells = jnp.arange(rows * cols, dtype=jnp.int32).reshape(rows, 1, cols)
    onehot = (sites[0][None, :, None] == cells).astype(jnp.float32)
    picked = dot(state, onehot, (0, 2), (0, 2), HIGHEST)
    tanh_picked = jnp.tanh(picked)
    observed = picked + 0.5 * tanh_picked
    sums = jnp.sum(state, axis=1)
    sums = jnp.concatenate([sums, jnp.zeros((-rows % 8, cols), jnp.float32)], axis=0)[None]
    obs_full, all_sums = gather_members(n_mem, [observed, sums], [0, 0], 3)
    average = jnp.sum(all_sums, axis=0)[:rows] / total
    observed_mean = jnp.sum(obs_full, axis=0) / total
    deviations = (state - average[:, None]) / scale
    anom_full = (obs_full - observed_mean) * precision / scale
    obs_anom = (observed - observed_mean) * precision / scale
    innovation = precision * (data - observed_mean)
    gram_rows = dot(obs_anom, anom_full, (1,), (1,))
    cross_rows = dot(deviations, cot_full, (0, 2), (0, 2))
    pull_rows = jnp.sum(obs_anom * innovation, axis=1)
    block = jnp.concatenate(
        [gram_rows, cross_rows, jnp.broadcast_to(pull_rows[:, None], (members, 128))], axis=1
    )
    near = 2 if n_space % 2 == 0 else 1
    block = block.reshape(n_space, members // n_space, -1)
    done = reduce_gather(n_space, n_mem, block, 4)
    done = jnp.transpose(done, (0, 2, 1, 3, 4)).reshape(total, -1)
    gram, cross, pull = done[:, :total], done[:, total : 2 * total], done[:, 2 * total]

    identity = jnp.eye(total, dtype=jnp.float32)
    system = identity + gram
    norm = jnp.sqrt(jnp.sum(system * system))
    root = jnp.sqrt(norm)
    approach = system / norm
    factor = 1.5 * identity - 0.5 * approach
    square = mm(factor, factor)
    transform = (1.5 * factor + mm(square, square - 1.5 * factor)) / root
    mid_pull = jnp.sum(transform * pull[None, :], axis=1)
    mean_weights = jnp.sum(transform * mid_pull[None, :], axis=1)
    mean_bar = jnp.sum(cross, axis=1)
    mid_bar = jnp.sum(transform * mean_bar[None, :], axis=1)
    pull_bar = jnp.sum(transform * mid_bar[None, :], axis=1)
    half_weight = (
        scale * cross + mean_bar[:, None] * mid_pull[None, :] + mid_bar[:, None] * pull[None, :]
    )
    weight_bar = 0.5 * (half_weight + half_weight.T)
    polar_bar = weight_bar / root
    scale_bar = -0.5 * jnp.sum(weight_bar * transform) / norm
    bar_square = mm(polar_bar, square)
    bar_mixed = mm(polar_bar, 2.0 * square - 1.5 * factor)
    square_bar = 0.5 * (bar_mixed + bar_mixed.T)
    bar_factor = mm(square_bar, factor)
    half_bar = 0.75 * polar_bar - 1.5 * 0.5 * bar_square + bar_factor
    approach_bar = -0.5 * (half_bar + half_bar.T)
    scale_bar = scale_bar - jnp.sum(approach_bar * approach) / norm
    sym_bar = 2.0 * (approach_bar + scale_bar * system) / norm

    offset = m * members
    take = lambda x: lax.dynamic_slice_in_dim(x, offset, members, 0)
    mix_rows = take(transform) + take(mean_weights)[:, None] / scale
    row_weights = jnp.sum(transform, axis=0) + jnp.sum(mean_weights) / scale
    mix_rows = mix_rows + ((1.0 - row_weights) / total)[None, :]
    sym_rows = take(sym_bar) - (jnp.sum(sym_bar, axis=0) / total)[None, :]
    sym_rows = sym_rows - (scale / total * pull_bar)[None, :]
    observed_bar = (precision / scale) * (
        mm(sym_rows, anom_full)
        + (take(pull_bar) - jnp.sum(pull_bar) / total)[:, None] * innovation[None, :]
    )
    picked_bar = observed_bar * (1.0 + 0.5 * (1.0 - tanh_picked * tanh_picked))
    field_bar = jnp.stack(
        [mm(mix_rows, cot_full[r]) + mm(picked_bar, onehot[r]) for r in range(rows)]
    )
    second_bar = sea_ext[2:-2] * field_bar
    low_bar, high_bar = halo(n_space, second_bar[-2:], second_bar[:2], 5)
    bar_ext = jnp.concatenate([low_bar, second_bar, high_bar], axis=0)
    first_bar = sea_ext[1:-1] * transpose_step(bar_ext, coef_ext)
    coef_part = coef_terms(second_bar, first_ext) + coef_terms(first_bar[1:-1], prior_ext[1:-1])
    (coef_all,) = gather_members(n_mem, [coef_part.reshape(1, 4 * rows, cols)], [0], 6)
    prior_grad = transpose_step(first_bar, coef_ext[:, 1:-1])
    coef_total = jnp.sum(coef_all, axis=0).reshape(4, rows, cols)
    return (
        jnp.transpose(prior_grad, (1, 0, 2)),
        coef_total / jnp.sqrt(jnp.float32(total)),
    )


def solution(mesh):
    placed = (
        P("mem", "space", None),
        P(None, "space", None),
        P("space", None),
        P("space", None),
        P("space"),
        P("space"),
        P("mem", "space", None),
    )
    return jax.shard_map(
        functools.partial(local, mesh.shape["space"], mesh.shape["mem"]),
        mesh=mesh,
        in_specs=placed,
        out_specs=(P("mem", "space", None), P(None, "space", None)),
        check_vma=False,
    )
```

```python
import functools
import jax
import jax.numpy as jnp
from jax import lax
from jax.experimental import pallas as pl
from jax.experimental.pallas import tpu as pltpu
from jax.sharding import PartitionSpec as P

MESH = pl.DeviceIdType.MESH
HIGH = lax.Precision.HIGH
HIGHEST = lax.Precision.HIGHEST
VMEM_SPEC = pl.BlockSpec(memory_space=pltpu.VMEM)


def dot(a, b, a_dims, b_dims, precision=HIGH):
    return lax.dot_general(
        a, b, ((a_dims, b_dims), ((), ())), precision=precision, preferred_element_type=jnp.float32
    )


def mm(a, b):
    return dot(a, b, (1,), (0,))


def remote(src, dst, send, recv, s, m):
    return pltpu.make_async_remote_copy(
        src_ref=src, dst_ref=dst, send_sem=send, recv_sem=recv, device_id=(s, m), device_id_type=MESH
    )


def params(ident):
    return pltpu.CompilerParams(collective_id=ident, has_side_effects=True)


def halo_body(n_space, last, first, low, high, send, recv, others):
    s, m = lax.axis_index("space"), lax.axis_index("mem")
    barrier = pltpu.get_barrier_semaphore()
    has_low, has_high = s > 0, s < n_space - 1

    @pl.when(has_low)
    def _():
        pl.semaphore_signal(barrier, inc=1, device_id=(s - 1, m), device_id_type=MESH)

    @pl.when(has_high)
    def _():
        pl.semaphore_signal(barrier, inc=1, device_id=(s + 1, m), device_id_type=MESH)

    for peer in others:
        pl.semaphore_signal(barrier, inc=1, device_id=peer, device_id_type=MESH)
    pl.semaphore_wait(
        barrier, has_low.astype(jnp.int32) + has_high.astype(jnp.int32) + len(others)
    )

    up = remote(last, low, send.at[0], recv.at[0], s + 1, m)
    down = remote(first, high, send.at[1], recv.at[1], s - 1, m)

    @pl.when(has_high)
    def _():
        up.start()

    @pl.when(has_low)
    def _():
        down.start()

    def finish():
        @pl.when(has_low)
        def _():
            up.wait_recv()
            down.wait_send()

        @pl.when(has_high)
        def _():
            down.wait_recv()
            up.wait_send()

    return finish


def masked(n_space, low, high):
    s = lax.axis_index("space")
    return jnp.where(s > 0, low, 0.0), jnp.where(s < n_space - 1, high, 0.0)


def halo(n_space, last, first, ident):
    def body(last_ref, first_ref, low, high, send, recv):
        halo_body(n_space, last_ref, first_ref, low, high, send, recv, [])()

    shape = jax.ShapeDtypeStruct(last.shape, last.dtype)
    low, high = pl.pallas_call(
        body,
        out_shape=(shape, shape),
        in_specs=[VMEM_SPEC] * 2,
        out_specs=(VMEM_SPEC,) * 2,
        scratch_shapes=[pltpu.SemaphoreType.DMA((2,)), pltpu.SemaphoreType.DMA((2,))],
        compiler_params=params(ident),
        name="halo",
    )(last, first)
    return masked(n_space, low, high)


def halo_gather(n_space, n_mem, last, first, block, ident):
    half = 2 if n_mem % 2 == 0 else 1
    wide = n_mem // half
    members = block.shape[1]

    def body(last_ref, first_ref, x, low, high, out, send, recv, own, p_send, p_recv, q_send, q_recv):
        s, m = lax.axis_index("space"), lax.axis_index("mem")
        p, q = m // half, lax.rem(m, half)
        across = [lax.rem(p + k, wide) * half + q for k in range(1, wide)]
        beside = [p * half + lax.rem(q + k, half) for k in range(1, half)]

        def part(which):
            return out.at[:, pl.ds(pl.multiple_of(which * members, members), members)]

        mine = pltpu.make_async_copy(x, part(m), own.at[0])
        mine.start()
        finish = halo_body(
            n_space, last_ref, first_ref, low, high, send, recv, [(s, to) for to in across + beside]
        )
        copies = []
        for k, to in enumerate(across):
            copies.append(remote(x, part(m), p_send.at[k], p_recv.at[k], s, to))
            copies[-1].start()
        hops = list(copies)
        for k, to in enumerate(beside):
            copies.append(remote(x, part(m), q_send.at[k, 0], q_recv.at[k, 0], s, to))
            copies[-1].start()
        for kp, hop in enumerate(hops):
            from_p = lax.rem(p + wide - kp - 1, wide)
            hop.wait_recv()
            piece = part(from_p * half + q)
            for k, to in enumerate(beside):
                copies.append(remote(piece, piece, q_send.at[k, kp + 1], q_recv.at[k, kp + 1], s, to))
                copies[-1].start()
        finish()
        mine.wait()
        for copy in copies[len(hops) :]:
            copy.wait_recv()
        for copy in copies:
            copy.wait_send()

    shape = jax.ShapeDtypeStruct(last.shape, last.dtype)
    full = list(block.shape)
    full[1] *= n_mem
    dma = pltpu.SemaphoreType.DMA
    low, high, out = pl.pallas_call(
        body,
        out_shape=(shape, shape, jax.ShapeDtypeStruct(tuple(full), block.dtype)),
        in_specs=[VMEM_SPEC] * 3,
        out_specs=(VMEM_SPEC,) * 3,
        scratch_shapes=[
            dma((2,)), dma((2,)), dma((1,)), dma((wide,)), dma((wide,)),
            dma((half, wide)), dma((half, wide)),
        ],
        compiler_params=params(ident),
        name="halo_gather",
    )(last, first, block)
    return *masked(n_space, low, high), out


def gather_members(n_mem, arrays, dims, ident):
    count = len(arrays)

    def body(*refs):
        ins, outs = refs[:count], refs[count : 2 * count]
        send, recv, own = refs[2 * count :]
        s, m = lax.axis_index("space"), lax.axis_index("mem")
        barrier = pltpu.get_barrier_semaphore()
        for k in range(1, n_mem):
            pl.semaphore_signal(
                barrier, inc=1, device_id=(s, lax.rem(m + k, n_mem)), device_id_type=MESH
            )

        def part(i, which):
            width = arrays[i].shape[dims[i]]
            where = [slice(None)] * arrays[i].ndim
            where[dims[i]] = pl.ds(pl.multiple_of(which * width, width), width)
            return outs[i].at[tuple(where)]

        mine = [pltpu.make_async_copy(ins[i], part(i, m), own.at[i]) for i in range(count)]
        for copy in mine:
            copy.start()
        pl.semaphore_wait(barrier, n_mem - 1)
        copies = []
        for k in range(1, n_mem):
            for i in range(count):
                copy = remote(
                    ins[i], part(i, m), send.at[i, k], recv.at[i, k], s, lax.rem(m + k, n_mem)
                )
                copy.start()
                copies.append(copy)
        for copy in copies:
            copy.wait()
        for copy in mine:
            copy.wait()

    shapes = []
    for array, dim in zip(arrays, dims):
        shape = list(array.shape)
        shape[dim] *= n_mem
        shapes.append(jax.ShapeDtypeStruct(tuple(shape), array.dtype))
    return pl.pallas_call(
        body,
        out_shape=tuple(shapes),
        in_specs=[VMEM_SPEC] * count,
        out_specs=(VMEM_SPEC,) * count,
        scratch_shapes=[
            pltpu.SemaphoreType.DMA((count, n_mem)),
            pltpu.SemaphoreType.DMA((count, n_mem)),
            pltpu.SemaphoreType.DMA((count,)),
        ],
        compiler_params=params(ident),
        name="gather_members",
    )(*arrays)


def reduce_gather(n_space, n_mem, rows, ident):
    pieces, height, width = rows.shape
    near = 2 if n_space % 2 == 0 else 1
    far = n_space // near
    half = 2 if n_mem % 2 == 0 else 1
    wide = n_mem // half
    group = max(1, far // 4)
    groups = far // group

    def body(x, out, buf, rs_send, rs_recv, own, a_send, a_recv, b_send, b_recv, p_send, p_recv, q_send, q_recv):
        s, m = lax.axis_index("space"), lax.axis_index("mem")
        a, b = s // near, lax.rem(s, near)
        p, q = m // half, lax.rem(m, half)
        barrier = pltpu.get_barrier_semaphore()
        peers = [(lax.rem(s + k, n_space), m) for k in range(1, n_space)]
        peers += [(s, lax.rem(p + k, wide) * half + q) for k in range(1, wide)]
        peers += [(s, p * half + lax.rem(q + k, half)) for k in range(1, half)]
        for peer in peers:
            pl.semaphore_signal(barrier, inc=1, device_id=peer, device_id_type=MESH)
        mine = pltpu.make_async_copy(x.at[s], buf.at[s], own.at[0])
        mine.start()
        pl.semaphore_wait(barrier, len(peers))
        scatter = []
        for k in range(1, n_space):
            to = lax.rem(s + k, n_space)
            copy = remote(x.at[to], buf.at[s], rs_send.at[k], rs_recv.at[k], to, m)
            copy.start()
            scatter.append(copy)
        mine.wait()
        for copy in scatter:
            copy.wait_recv()
        total = buf[0]
        for k in range(1, n_space):
            total = total + buf[k]
        out[m, a, b] = total

        waits = list(scatter)
        stage_a = []
        for k in range(1, far):
            to = lax.rem(a + k, far)
            copy = remote(
                out.at[m, a, b], out.at[m, a, b], a_send.at[k], a_recv.at[k], to * near + b, m
            )
            copy.start()
            stage_a.append(copy)
        if group == 1:
            a_steps = [([], a)] + [([stage_a[k - 1]], lax.rem(a + far - k, far)) for k in range(1, far)]
        else:
            a_steps = [(stage_a if g == 0 else [], g * group) for g in range(groups)]
        steps_b = []
        for index, (needs, start) in enumerate(a_steps):
            for copy in needs:
                copy.wait_recv()
            steps_b.append((start, index))
            flow(
                out, s, m, b, p, q, start, index, 0, group, near, half, wide,
                b_send, b_recv, p_send, p_recv, q_send, q_recv, waits,
            )
        waits += stage_a
        for start, index in steps_b:
            pend = []
            for kb in range(1, near):
                pend.append((start, index, kb))
            for start_, index_, kb in pend:
                from_b = lax.rem(b + near - kb, near)
                piece = out.at[m, pl.ds(start_, group), from_b]
                remote(piece, piece, b_send.at[kb, index_], b_recv.at[kb, index_], s, m).wait_recv()
                flow(
                    out, s, m, from_b, p, q, start_, index_, kb, group, near, half, wide,
                    None, None, p_send, p_recv, q_send, q_recv, waits,
                )
        for start, index in steps_b:
            for kb in range(near):
                which_b = lax.rem(b + near - kb, near)
                for kp in range(1, wide):
                    from_p = lax.rem(p + wide - kp, wide)
                    piece = out.at[from_p * half + q, pl.ds(start, group), which_b]
                    remote(
                        piece, piece, p_send.at[kp, kb, index], p_recv.at[kp, kb, index], s, m
                    ).wait_recv()
                    for kq in range(1, half):
                        to_q = lax.rem(q + kq, half)
                        copy = remote(
                            piece, piece, q_send.at[kq, kp, kb, index], q_recv.at[kq, kp, kb, index],
                            s, p * half + to_q,
                        )
                        copy.start()
                        waits.append(copy)
        for start, index in steps_b:
            for kb in range(near):
                which_b = lax.rem(b + near - kb, near)
                for kp in range(wide):
                    from_p = lax.rem(p + wide - kp, wide)
                    for kq in range(1, half):
                        from_q = lax.rem(q + half - kq, half)
                        piece = out.at[from_p * half + from_q, pl.ds(start, group), which_b]
                        remote(
                            piece, piece, q_send.at[kq, kp, kb, index],
                            q_recv.at[kq, kp, kb, index], s, m,
                        ).wait_recv()
        for copy in waits:
            copy.wait_send()

    def flow(
        out, s, m, which_b, p, q, start, index, kb, group, near, half, wide,
        b_send, b_recv, p_send, p_recv, q_send, q_recv, waits,
    ):
        piece = out.at[m, pl.ds(start, group), which_b]
        for kp in range(1, wide):
            copy = remote(
                piece, piece, p_send.at[kp, kb, index], p_recv.at[kp, kb, index],
                s, lax.rem(p + kp, wide) * half + q,
            )
            copy.start()
            waits.append(copy)
        if b_send is not None:
            for k in range(1, near):
                to = (s // near) * near + lax.rem(which_b + k, near)
                copy = remote(piece, piece, b_send.at[k, index], b_recv.at[k, index], to, m)
                copy.start()
                waits.append(copy)
        for kq in range(1, half):
            copy = remote(
                piece, piece, q_send.at[kq, 0, kb, index], q_recv.at[kq, 0, kb, index],
                s, p * half + lax.rem(q + kq, half),
            )
            copy.start()
            waits.append(copy)

    dma = pltpu.SemaphoreType.DMA
    out = pl.pallas_call(
        body,
        out_shape=jax.ShapeDtypeStruct((n_mem, far, near, height, width), rows.dtype),
        in_specs=[VMEM_SPEC],
        out_specs=VMEM_SPEC,
        scratch_shapes=[
            pltpu.VMEM(rows.shape, rows.dtype),
            dma((n_space,)), dma((n_space,)), dma((1,)),
            dma((far,)), dma((far,)),
            dma((near, groups)), dma((near, groups)),
            dma((wide, near, groups)), dma((wide, near, groups)),
            dma((half, wide, near, groups)), dma((half, wide, near, groups)),
        ],
        compiler_params=params(ident),
        name="reduce_gather",
    )(rows)
    return out


def split(x):
    lead = x.astype(jnp.bfloat16)
    return lead, (x - lead.astype(jnp.float32)).astype(jnp.bfloat16)


def mm3(a, b):
    plain = lambda x, y: jnp.dot(x, y, preferred_element_type=jnp.float32)
    return plain(a[0], b[0]) + (plain(a[0], b[1]) + plain(a[1], b[0]))


def analyse(done, cot_full, anom_full, innovation, precision, tanh_picked, onehot, sea, members):
    total = done.shape[0]
    rows, _, cols = cot_full.shape

    def body(done, cot, anom, innov, prec, tanh, hot, sea, out, f_ref, f2_ref, t_ref, s_ref, u_ref, y_ref, v_ref):
        scale = jnp.sqrt(jnp.float32(total - 1))
        offset = pl.multiple_of(lax.axis_index("mem") * members, members)
        mine = pl.ds(offset, members)
        diagonal = lax.broadcasted_iota(jnp.int32, (total, total), 0) == lax.broadcasted_iota(
            jnp.int32, (total, total), 1
        )
        identity = diagonal.astype(jnp.float32)
        whole = lambda x: jnp.sum(jnp.sum(x, axis=0, keepdims=True), axis=1, keepdims=True)
        system = identity + done[:, :total]
        norm = jnp.sqrt(whole(system * system))
        root = jnp.sqrt(norm)
        f_ref[...] = 1.5 * identity - 0.5 * (system / norm)
        f_split = split(f_ref[...])
        f2_ref[...] = mm3(f_split, f_split)
        f2_split = split(f2_ref[...])
        t_ref[...] = (
            1.5 * f_ref[...] + mm3(f2_split, split(f2_ref[...] - 1.5 * f_ref[...]))
        ) / root
        t_split = split(t_ref[...])
        pull = done[:, 2 * total :]
        mean_bar = jnp.sum(done[:, total : 2 * total], axis=1, keepdims=True)
        first = mm3(t_split, split(jnp.concatenate([pull, jnp.broadcast_to(mean_bar, pull.shape)], axis=1)))
        v_ref[...] = mm3(t_split, split(first))
        width = pull.shape[1]
        row = lambda x: x.T[:1]
        s_ref[...] = (
            scale * done[:, total : 2 * total]
            + mean_bar * row(first[:, :width])
            + first[:, width : width + 1] * row(pull)
        )
        weight = 0.5 * (s_ref[...] + s_ref[...].T)
        scale_bar = -0.5 * whole(weight * t_ref[...]) / norm
        s_ref[...] = weight / root
        s_split = split(s_ref[...])
        u_ref[...] = mm3(s_split, f2_split)
        y_ref[...] = mm3(s_split, split(2.0 * f2_ref[...] - 1.5 * f_ref[...]))
        y_ref[...] = 0.5 * (y_ref[...] + y_ref[...].T)
        approach = 1.5 * s_ref[...] - 1.5 * u_ref[...]
        approach = whole(
            approach * (3.0 * identity - 2.0 * f_ref[...])
            + 2.0 * y_ref[...] * (3.0 * f_ref[...] - 2.0 * f2_ref[...])
        )
        scale_bar = scale_bar + 0.5 * approach / norm

        centred = lambda ref: ref[mine, :] - jnp.sum(ref[...], axis=0, keepdims=True) / total
        f_mine = centred(f_ref)
        bar = 1.5 * centred(s_ref) - 0.75 * (centred(u_ref) + mm3(split(centred(f2_ref)), s_split))
        bar = bar + mm3(split(centred(y_ref)), f_split) + mm3(split(f_mine), split(y_ref[...]))
        unit = (
            lax.broadcasted_iota(jnp.int32, (members, total), 0) + offset
            == lax.broadcasted_iota(jnp.int32, (members, total), 1)
        ).astype(jnp.float32) - 1.0 / total
        system_mine = norm * (3.0 * unit - 2.0 * f_mine)
        sym = 2.0 * (-0.5 * bar + scale_bar * system_mine) / norm
        pull_bar = v_ref[:, width:]
        sym = sym - (scale / total) * row(pull_bar)
        pull_mine = v_ref[mine, width:][:, :1] - jnp.sum(pull_bar[:, :1], axis=0, keepdims=True) / total
        mean_weights = v_ref[:, :1]
        mix = t_ref[mine, :] + v_ref[mine, :width][:, :1] / scale
        row_weights = (
            jnp.sum(t_ref[...], axis=0, keepdims=True)
            + jnp.sum(mean_weights, axis=0, keepdims=True) / scale
        )
        mix = mix + (1.0 - row_weights) / total
        observed = (prec[...] / scale) * (mm3(split(sym), split(anom[...])) + pull_mine * innov[...])
        picked = observed * (1.0 + 0.5 * (1.0 - tanh[...] * tanh[...]))
        mix_split, picked_split = split(mix), split(picked)
        for r in range(rows):
            mark = hot[r].astype(jnp.bfloat16)
            spread = jnp.dot(picked_split[0], mark, preferred_element_type=jnp.float32) + jnp.dot(
                picked_split[1], mark, preferred_element_type=jnp.float32
            )
            out[r] = sea[r] * (mm3(mix_split, split(cot[r])) + spread)

    square = pltpu.VMEM((total, total), jnp.float32)
    return pl.pallas_call(
        body,
        out_shape=jax.ShapeDtypeStruct((rows, members, cols), jnp.float32),
        in_specs=[VMEM_SPEC] * 8,
        out_specs=VMEM_SPEC,
        scratch_shapes=[square] * 6 + [pltpu.VMEM((total, 2 * (done.shape[1] - 2 * total)), jnp.float32)],
        compiler_params=pltpu.CompilerParams(vmem_limit_bytes=60 * 1024 * 1024),
        cost_estimate=pl.CostEstimate(flops=10 * total**3, bytes_accessed=8 * total**2, transcendentals=0),
        name="analyse",
    )(done, cot_full, anom_full, innovation, precision, tanh_picked, onehot, sea)


def neighbours(ext):
    center, north, south = ext[1:-1], ext[:-2], ext[2:]
    border = jnp.zeros_like(center[..., :1])
    west = jnp.concatenate([border, center[..., :-1]], axis=-1)
    east = jnp.concatenate([center[..., 1:], border], axis=-1)
    return center, north, south, west, east


def substep(ext, coef, sea):
    center, north, south, west, east = neighbours(ext)
    return sea * (
        center
        + coef[0] * (north - center)
        + coef[1] * (south - center)
        + coef[2] * (west - center)
        + coef[3] * (east - center)
    )


def transpose_step(ext, coef_ext):
    center = ext[1:-1]
    inner = coef_ext[:, 1:-1]
    from_south = coef_ext[0, 2:] * ext[2:]
    from_north = coef_ext[1, :-2] * ext[:-2]
    border = jnp.zeros_like(center[..., :1])
    from_east = jnp.concatenate([(inner[2] * center)[..., 1:], border], axis=-1)
    from_west = jnp.concatenate([border, (inner[3] * center)[..., :-1]], axis=-1)
    keeping = 1.0 - inner[0] - inner[1] - inner[2] - inner[3]
    return center * keeping + from_south + from_north + from_east + from_west


def coef_terms(weight, ext):
    center, north, south, west, east = neighbours(ext)
    return jnp.stack(
        [jnp.sum(weight * (side - center), axis=1) for side in (north, south, west, east)]
    )


def local(n_space, n_mem, prior, stencil, sea_mask, sites, data, precision, cotangent):
    members, rows, cols = prior.shape
    total = members * n_mem
    scale = jnp.sqrt(jnp.float32(total - 1))
    m = lax.axis_index("mem")
    prior_t = jnp.transpose(prior, (1, 0, 2))
    cot_t = jnp.transpose(cotangent, (1, 0, 2))
    aux = jnp.concatenate(
        [
            jnp.transpose(stencil, (1, 0, 2)),
            sea_mask.astype(jnp.float32)[:, None],
            jnp.zeros((rows, 3, cols), jnp.float32),
        ],
        axis=1,
    )
    packed = jnp.concatenate([prior_t, aux], axis=1)
    low, high, cot_full = halo_gather(n_space, n_mem, packed[-2:], packed[:2], cot_t, 1)
    ext = jnp.concatenate([low, packed, high], axis=0)
    prior_ext = ext[:, :members]
    coef_ext = jnp.transpose(ext[:, members : members + 4], (1, 0, 2))[:, :, None]
    sea_ext = ext[:, members + 4][:, None]
    first_ext = substep(prior_ext, coef_ext[:, 1:-1], sea_ext[1:-1])
    state = substep(first_ext, coef_ext[:, 2:-2], sea_ext[2:-2])
    cells = jnp.arange(rows * cols, dtype=jnp.int32).reshape(rows, 1, cols)
    onehot = (sites[0][None, :, None] == cells).astype(jnp.float32)
    picked = dot(state, onehot, (0, 2), (0, 2), HIGHEST)
    tanh_picked = jnp.tanh(picked)
    observed = picked + 0.5 * tanh_picked
    sums = jnp.sum(state, axis=1)
    sums = jnp.concatenate([sums, jnp.zeros((-rows % 8, cols), jnp.float32)], axis=0)[None]
    obs_full, all_sums = gather_members(n_mem, [observed, sums], [0, 0], 3)
    average = jnp.sum(all_sums, axis=0)[:rows] / total
    observed_mean = jnp.sum(obs_full, axis=0) / total
    deviations = (state - average[:, None]) / scale
    anom_full = (obs_full - observed_mean) * precision / scale
    obs_anom = (observed - observed_mean) * precision / scale
    innovation = precision * (data - observed_mean)
    gram_rows = dot(obs_anom, anom_full, (1,), (1,))
    cross_rows = dot(deviations, cot_full, (0, 2), (0, 2))
    pull_rows = jnp.sum(obs_anom * innovation, axis=1)
    block = jnp.concatenate(
        [gram_rows, cross_rows, jnp.broadcast_to(pull_rows[:, None], (members, 128))], axis=1
    )
    block = block.reshape(n_space, members // n_space, -1)
    done = reduce_gather(n_space, n_mem, block, 4)
    done = done.reshape(total, -1)
    second_bar = analyse(
        done, cot_full, anom_full, innovation[None], precision[None], tanh_picked,
        onehot, sea_ext[2:-2], members,
    )
    low_bar, high_bar = halo(n_space, second_bar[-2:], second_bar[:2], 5)
    bar_ext = jnp.concatenate([low_bar, second_bar, high_bar], axis=0)
    first_bar = sea_ext[1:-1] * transpose_step(bar_ext, coef_ext)
    coef_part = coef_terms(second_bar, first_ext) + coef_terms(first_bar[1:-1], prior_ext[1:-1])
    (coef_all,) = gather_members(n_mem, [coef_part.reshape(1, 4 * rows, cols)], [0], 6)
    prior_grad = transpose_step(first_bar, coef_ext[:, 1:-1])
    coef_total = jnp.sum(coef_all, axis=0).reshape(4, rows, cols)
    return (
        jnp.transpose(prior_grad, (1, 0, 2)),
        coef_total / jnp.sqrt(jnp.float32(total)),
    )


def solution(mesh):
    placed = (
        P("mem", "space", None),
        P(None, "space", None),
        P("space", None),
        P("space", None),
        P("space"),
        P("space"),
        P("mem", "space", None),
    )
    return jax.shard_map(
        functools.partial(local, mesh.shape["space"], mesh.shape["mem"]),
        mesh=mesh,
        in_specs=placed,
        out_specs=(P("mem", "space", None), P(None, "space", None)),
        check_vma=False,
    )
```

```python
import functools
import jax
import jax.numpy as jnp
from jax import lax
from jax.experimental import pallas as pl
from jax.experimental.pallas import tpu as pltpu
from jax.sharding import PartitionSpec as P

MESH = pl.DeviceIdType.MESH
HIGH = lax.Precision.HIGH
HIGHEST = lax.Precision.HIGHEST
VMEM_SPEC = pl.BlockSpec(memory_space=pltpu.VMEM)


def dot(a, b, a_dims, b_dims, precision=HIGH):
    return lax.dot_general(
        a, b, ((a_dims, b_dims), ((), ())), precision=precision, preferred_element_type=jnp.float32
    )


def mm(a, b):
    return dot(a, b, (1,), (0,))


def remote(src, dst, send, recv, s, m):
    return pltpu.make_async_remote_copy(
        src_ref=src, dst_ref=dst, send_sem=send, recv_sem=recv, device_id=(s, m), device_id_type=MESH
    )


def params(ident):
    return pltpu.CompilerParams(collective_id=ident, has_side_effects=True)


def halo_body(n_space, last, first, low, high, send, recv, others):
    s, m = lax.axis_index("space"), lax.axis_index("mem")
    barrier = pltpu.get_barrier_semaphore()
    has_low, has_high = s > 0, s < n_space - 1

    @pl.when(has_low)
    def _():
        pl.semaphore_signal(barrier, inc=1, device_id=(s - 1, m), device_id_type=MESH)

    @pl.when(has_high)
    def _():
        pl.semaphore_signal(barrier, inc=1, device_id=(s + 1, m), device_id_type=MESH)

    for peer in others:
        pl.semaphore_signal(barrier, inc=1, device_id=peer, device_id_type=MESH)
    pl.semaphore_wait(
        barrier, has_low.astype(jnp.int32) + has_high.astype(jnp.int32) + len(others)
    )

    up = remote(last, low, send.at[0], recv.at[0], s + 1, m)
    down = remote(first, high, send.at[1], recv.at[1], s - 1, m)

    @pl.when(has_high)
    def _():
        up.start()

    @pl.when(has_low)
    def _():
        down.start()

    def finish():
        @pl.when(has_low)
        def _():
            up.wait_recv()
            down.wait_send()

        @pl.when(has_high)
        def _():
            down.wait_recv()
            up.wait_send()

    return finish


def halo(n_space, last, first, ident):
    def body(last_ref, first_ref, low, high, send, recv):
        halo_body(n_space, last_ref, first_ref, low, high, send, recv, [])()

    shape = jax.ShapeDtypeStruct(last.shape, last.dtype)
    low, high = pl.pallas_call(
        body,
        out_shape=(shape, shape),
        in_specs=[VMEM_SPEC] * 2,
        out_specs=(VMEM_SPEC,) * 2,
        scratch_shapes=[pltpu.SemaphoreType.DMA((2,)), pltpu.SemaphoreType.DMA((2,))],
        compiler_params=params(ident),
        name="halo",
    )(last, first)
    return low, high


def halo_gather(n_space, n_mem, last, first, block, ident):
    half = 2 if n_mem % 2 == 0 else 1
    wide = n_mem // half
    members = block.shape[1]

    def body(last_ref, first_ref, x, low, high, out, send, recv, own, p_send, p_recv, q_send, q_recv):
        s, m = lax.axis_index("space"), lax.axis_index("mem")
        p, q = m // half, lax.rem(m, half)
        across = [lax.rem(p + k, wide) * half + q for k in range(1, wide)]
        beside = [p * half + lax.rem(q + k, half) for k in range(1, half)]

        def part(which):
            return out.at[:, pl.ds(pl.multiple_of(which * members, members), members)]

        mine = pltpu.make_async_copy(x, part(m), own.at[0])
        mine.start()
        finish = halo_body(
            n_space, last_ref, first_ref, low, high, send, recv, [(s, to) for to in across + beside]
        )
        copies = []
        for k, to in enumerate(across):
            copies.append(remote(x, part(m), p_send.at[k], p_recv.at[k], s, to))
            copies[-1].start()
        hops = list(copies)
        for k, to in enumerate(beside):
            copies.append(remote(x, part(m), q_send.at[k, 0], q_recv.at[k, 0], s, to))
            copies[-1].start()
        for kp, hop in enumerate(hops):
            from_p = lax.rem(p + wide - kp - 1, wide)
            hop.wait_recv()
            piece = part(from_p * half + q)
            for k, to in enumerate(beside):
                copies.append(remote(piece, piece, q_send.at[k, kp + 1], q_recv.at[k, kp + 1], s, to))
                copies[-1].start()
        finish()
        mine.wait()
        for copy in copies[len(hops) :]:
            copy.wait_recv()
        for copy in copies:
            copy.wait_send()

    shape = jax.ShapeDtypeStruct(last.shape, last.dtype)
    full = list(block.shape)
    full[1] *= n_mem
    dma = pltpu.SemaphoreType.DMA
    low, high, out = pl.pallas_call(
        body,
        out_shape=(shape, shape, jax.ShapeDtypeStruct(tuple(full), block.dtype)),
        in_specs=[VMEM_SPEC] * 3,
        out_specs=(VMEM_SPEC,) * 3,
        scratch_shapes=[
            dma((2,)), dma((2,)), dma((1,)), dma((wide,)), dma((wide,)),
            dma((half, wide)), dma((half, wide)),
        ],
        compiler_params=params(ident),
        name="halo_gather",
    )(last, first, block)
    return low, high, out


def gather_members(n_mem, arrays, dims, ident):
    count = len(arrays)

    def body(*refs):
        ins, outs = refs[:count], refs[count : 2 * count]
        send, recv, own = refs[2 * count :]
        s, m = lax.axis_index("space"), lax.axis_index("mem")
        barrier = pltpu.get_barrier_semaphore()
        for k in range(1, n_mem):
            pl.semaphore_signal(
                barrier, inc=1, device_id=(s, lax.rem(m + k, n_mem)), device_id_type=MESH
            )

        def part(i, which):
            width = arrays[i].shape[dims[i]]
            where = [slice(None)] * arrays[i].ndim
            where[dims[i]] = pl.ds(pl.multiple_of(which * width, width), width)
            return outs[i].at[tuple(where)]

        mine = [pltpu.make_async_copy(ins[i], part(i, m), own.at[i]) for i in range(count)]
        for copy in mine:
            copy.start()
        pl.semaphore_wait(barrier, n_mem - 1)
        copies = []
        for k in range(1, n_mem):
            for i in range(count):
                copy = remote(
                    ins[i], part(i, m), send.at[i, k], recv.at[i, k], s, lax.rem(m + k, n_mem)
                )
                copy.start()
                copies.append(copy)
        for copy in copies:
            copy.wait()
        for copy in mine:
            copy.wait()

    shapes = []
    for array, dim in zip(arrays, dims):
        shape = list(array.shape)
        shape[dim] *= n_mem
        shapes.append(jax.ShapeDtypeStruct(tuple(shape), array.dtype))
    return pl.pallas_call(
        body,
        out_shape=tuple(shapes),
        in_specs=[VMEM_SPEC] * count,
        out_specs=(VMEM_SPEC,) * count,
        scratch_shapes=[
            pltpu.SemaphoreType.DMA((count, n_mem)),
            pltpu.SemaphoreType.DMA((count, n_mem)),
            pltpu.SemaphoreType.DMA((count,)),
        ],
        compiler_params=params(ident),
        name="gather_members",
    )(*arrays)


def reduce_gather(n_space, n_mem, rows, ident):
    pieces, height, width = rows.shape
    near = 2 if n_space % 2 == 0 else 1
    far = n_space // near
    half = 2 if n_mem % 2 == 0 else 1
    wide = n_mem // half
    group = max(1, far // 4)
    groups = far // group

    def body(x, out, buf, rs_send, rs_recv, own, a_send, a_recv, b_send, b_recv, p_send, p_recv, q_send, q_recv):
        s, m = lax.axis_index("space"), lax.axis_index("mem")
        a, b = s // near, lax.rem(s, near)
        p, q = m // half, lax.rem(m, half)
        barrier = pltpu.get_barrier_semaphore()
        peers = [(lax.rem(s + k, n_space), m) for k in range(1, n_space)]
        peers += [(s, lax.rem(p + k, wide) * half + q) for k in range(1, wide)]
        peers += [(s, p * half + lax.rem(q + k, half)) for k in range(1, half)]
        for peer in peers:
            pl.semaphore_signal(barrier, inc=1, device_id=peer, device_id_type=MESH)
        mine = pltpu.make_async_copy(x.at[s], buf.at[s], own.at[0])
        mine.start()
        pl.semaphore_wait(barrier, len(peers))
        scatter = []
        for k in range(1, n_space):
            to = lax.rem(s + k, n_space)
            copy = remote(x.at[to], buf.at[s], rs_send.at[k], rs_recv.at[k], to, m)
            copy.start()
            scatter.append(copy)
        mine.wait()
        for copy in scatter:
            copy.wait_recv()
        total = buf[0]
        for k in range(1, n_space):
            total = total + buf[k]
        out[m, a, b] = total

        waits = list(scatter)
        stage_a = []
        for k in range(1, far):
            to = lax.rem(a + k, far)
            copy = remote(
                out.at[m, a, b], out.at[m, a, b], a_send.at[k], a_recv.at[k], to * near + b, m
            )
            copy.start()
            stage_a.append(copy)
        if group == 1:
            a_steps = [([], a)] + [([stage_a[k - 1]], lax.rem(a + far - k, far)) for k in range(1, far)]
        else:
            a_steps = [(stage_a if g == 0 else [], g * group) for g in range(groups)]
        steps_b = []
        for index, (needs, start) in enumerate(a_steps):
            for copy in needs:
                copy.wait_recv()
            steps_b.append((start, index))
            flow(
                out, s, m, b, p, q, start, index, 0, group, near, half, wide,
                b_send, b_recv, p_send, p_recv, q_send, q_recv, waits,
            )
        waits += stage_a
        for start, index in steps_b:
            pend = []
            for kb in range(1, near):
                pend.append((start, index, kb))
            for start_, index_, kb in pend:
                from_b = lax.rem(b + near - kb, near)
                piece = out.at[m, pl.ds(start_, group), from_b]
                remote(piece, piece, b_send.at[kb, index_], b_recv.at[kb, index_], s, m).wait_recv()
                flow(
                    out, s, m, from_b, p, q, start_, index_, kb, group, near, half, wide,
                    None, None, p_send, p_recv, q_send, q_recv, waits,
                )
        for start, index in steps_b:
            for kb in range(near):
                which_b = lax.rem(b + near - kb, near)
                for kp in range(1, wide):
                    from_p = lax.rem(p + wide - kp, wide)
                    piece = out.at[from_p * half + q, pl.ds(start, group), which_b]
                    remote(
                        piece, piece, p_send.at[kp, kb, index], p_recv.at[kp, kb, index], s, m
                    ).wait_recv()
                    for kq in range(1, half):
                        to_q = lax.rem(q + kq, half)
                        copy = remote(
                            piece, piece, q_send.at[kq, kp, kb, index], q_recv.at[kq, kp, kb, index],
                            s, p * half + to_q,
                        )
                        copy.start()
                        waits.append(copy)
        for start, index in steps_b:
            for kb in range(near):
                which_b = lax.rem(b + near - kb, near)
                for kp in range(wide):
                    from_p = lax.rem(p + wide - kp, wide)
                    for kq in range(1, half):
                        from_q = lax.rem(q + half - kq, half)
                        piece = out.at[from_p * half + from_q, pl.ds(start, group), which_b]
                        remote(
                            piece, piece, q_send.at[kq, kp, kb, index],
                            q_recv.at[kq, kp, kb, index], s, m,
                        ).wait_recv()
        for copy in waits:
            copy.wait_send()

    def flow(
        out, s, m, which_b, p, q, start, index, kb, group, near, half, wide,
        b_send, b_recv, p_send, p_recv, q_send, q_recv, waits,
    ):
        piece = out.at[m, pl.ds(start, group), which_b]
        for kp in range(1, wide):
            copy = remote(
                piece, piece, p_send.at[kp, kb, index], p_recv.at[kp, kb, index],
                s, lax.rem(p + kp, wide) * half + q,
            )
            copy.start()
            waits.append(copy)
        if b_send is not None:
            for k in range(1, near):
                to = (s // near) * near + lax.rem(which_b + k, near)
                copy = remote(piece, piece, b_send.at[k, index], b_recv.at[k, index], to, m)
                copy.start()
                waits.append(copy)
        for kq in range(1, half):
            copy = remote(
                piece, piece, q_send.at[kq, 0, kb, index], q_recv.at[kq, 0, kb, index],
                s, p * half + lax.rem(q + kq, half),
            )
            copy.start()
            waits.append(copy)

    dma = pltpu.SemaphoreType.DMA
    out = pl.pallas_call(
        body,
        out_shape=jax.ShapeDtypeStruct((n_mem, far, near, height, width), rows.dtype),
        in_specs=[VMEM_SPEC],
        out_specs=VMEM_SPEC,
        scratch_shapes=[
            pltpu.VMEM(rows.shape, rows.dtype),
            dma((n_space,)), dma((n_space,)), dma((1,)),
            dma((far,)), dma((far,)),
            dma((near, groups)), dma((near, groups)),
            dma((wide, near, groups)), dma((wide, near, groups)),
            dma((half, wide, near, groups)), dma((half, wide, near, groups)),
        ],
        compiler_params=params(ident),
        name="reduce_gather",
    )(rows)
    return out


def split(x):
    lead = x.astype(jnp.bfloat16)
    return lead, (x - lead.astype(jnp.float32)).astype(jnp.bfloat16)


def mm3(a, b):
    plain = lambda x, y: jnp.dot(x, y, preferred_element_type=jnp.float32)
    return plain(a[0], b[0]) + (plain(a[0], b[1]) + plain(a[1], b[0]))


def analyse(done, cot_full, anom_full, innovation, precision, tanh_picked, onehot, sea, members):
    total = done.shape[0]
    rows, _, cols = cot_full.shape

    def body(done, cot, anom, innov, prec, tanh, hot, sea, out, f_ref, f2_ref, t_ref, s_ref, u_ref, y_ref, v_ref):
        scale = jnp.sqrt(jnp.float32(total - 1))
        offset = pl.multiple_of(lax.axis_index("mem") * members, members)
        mine = pl.ds(offset, members)
        diagonal = lax.broadcasted_iota(jnp.int32, (total, total), 0) == lax.broadcasted_iota(
            jnp.int32, (total, total), 1
        )
        identity = diagonal.astype(jnp.float32)
        whole = lambda x: jnp.sum(jnp.sum(x, axis=0, keepdims=True), axis=1, keepdims=True)
        for p in range(4):
            here, there = pl.ds(p * members, members), pl.ds((p + 1) % 4 * members, members)
            s_ref[here, here] = done[here, total : total + members]
            edge = done[here, total + members : total + 2 * members]
            s_ref[here, there] = edge
            s_ref[there, here] = edge.T
        for p in range(2):
            here, there = pl.ds(p * members, members), pl.ds((p + 2) * members, members)
            pair = slice(total + 2 * members, total + 2 * members + members // 2)
            edge = jnp.concatenate([done[here, pair], done[there, pair]], axis=1)
            s_ref[here, there] = edge
            s_ref[there, here] = edge.T
        system = identity + s_ref[...]
        norm = jnp.sqrt(whole(system * system))
        root = jnp.sqrt(norm)
        f_ref[...] = 1.5 * identity - 0.5 * (system / norm)
        f_split = split(f_ref[...])
        f2_ref[...] = mm3(f_split, f_split)
        f2_split = split(f2_ref[...])
        t_ref[...] = (
            1.5 * f_ref[...] + mm3(f2_split, split(f2_ref[...] - 1.5 * f_ref[...]))
        ) / root
        t_split = split(t_ref[...])
        pull = jnp.broadcast_to(done[:, total + 3 * members - 1 :], (total, 128))
        mean_bar = jnp.sum(done[:, :total], axis=1, keepdims=True)
        first = mm3(t_split, split(jnp.concatenate([pull, jnp.broadcast_to(mean_bar, pull.shape)], axis=1)))
        v_ref[...] = mm3(t_split, split(first))
        width = pull.shape[1]
        row = lambda x: x.T[:1]
        s_ref[...] = (
            scale * done[:, :total]
            + mean_bar * row(first[:, :width])
            + first[:, width : width + 1] * row(pull)
        )
        weight = 0.5 * (s_ref[...] + s_ref[...].T)
        scale_bar = -0.5 * whole(weight * t_ref[...]) / norm
        s_ref[...] = weight / root
        s_split = split(s_ref[...])
        u_ref[...] = mm3(s_split, f2_split)
        y_ref[...] = mm3(s_split, split(2.0 * f2_ref[...] - 1.5 * f_ref[...]))
        y_ref[...] = 0.5 * (y_ref[...] + y_ref[...].T)
        approach = 1.5 * s_ref[...] - 1.5 * u_ref[...]
        approach = whole(
            approach * (3.0 * identity - 2.0 * f_ref[...])
            + 2.0 * y_ref[...] * (3.0 * f_ref[...] - 2.0 * f2_ref[...])
        )
        scale_bar = scale_bar + 0.5 * approach / norm

        centred = lambda ref: ref[mine, :] - jnp.sum(ref[...], axis=0, keepdims=True) / total
        f_mine = centred(f_ref)
        bar = 1.5 * centred(s_ref) - 0.75 * (centred(u_ref) + mm3(split(centred(f2_ref)), s_split))
        bar = bar + mm3(split(centred(y_ref)), f_split) + mm3(split(f_mine), split(y_ref[...]))
        unit = (
            lax.broadcasted_iota(jnp.int32, (members, total), 0) + offset
            == lax.broadcasted_iota(jnp.int32, (members, total), 1)
        ).astype(jnp.float32) - 1.0 / total
        system_mine = norm * (3.0 * unit - 2.0 * f_mine)
        sym = 2.0 * (-0.5 * bar + scale_bar * system_mine) / norm
        pull_bar = v_ref[:, width:]
        sym = sym - (scale / total) * row(pull_bar)
        pull_mine = v_ref[mine, width:][:, :1] - jnp.sum(pull_bar[:, :1], axis=0, keepdims=True) / total
        mean_weights = v_ref[:, :1]
        mix = t_ref[mine, :] + v_ref[mine, :width][:, :1] / scale
        row_weights = (
            jnp.sum(t_ref[...], axis=0, keepdims=True)
            + jnp.sum(mean_weights, axis=0, keepdims=True) / scale
        )
        mix = mix + (1.0 - row_weights) / total
        observed = (prec[...] / scale) * (mm3(split(sym), split(anom[...])) + pull_mine * innov[...])
        picked = observed * (1.0 + 0.5 * (1.0 - tanh[...] * tanh[...]))
        mix_split, picked_split = split(mix), split(picked)
        for r in range(rows):
            mark = hot[r].astype(jnp.bfloat16)
            spread = jnp.dot(picked_split[0], mark, preferred_element_type=jnp.float32) + jnp.dot(
                picked_split[1], mark, preferred_element_type=jnp.float32
            )
            out[r] = sea[r] * (mm3(mix_split, split(cot[r])) + spread)

    square = pltpu.VMEM((total, total), jnp.float32)
    return pl.pallas_call(
        body,
        out_shape=jax.ShapeDtypeStruct((rows, members, cols), jnp.float32),
        in_specs=[VMEM_SPEC] * 8,
        out_specs=VMEM_SPEC,
        scratch_shapes=[square] * 6 + [pltpu.VMEM((total, 256), jnp.float32)],
        compiler_params=pltpu.CompilerParams(vmem_limit_bytes=60 * 1024 * 1024),
        cost_estimate=pl.CostEstimate(flops=10 * total**3, bytes_accessed=8 * total**2, transcendentals=0),
        name="analyse",
    )(done, cot_full, anom_full, innovation, precision, tanh_picked, onehot, sea)


def side(x, step):
    lane = lax.broadcasted_iota(jnp.int32, x.shape, 1)
    last = x.shape[1] - 1
    if step > 0:
        return jnp.where(lane == 0, 0.0, pltpu.roll(x, 1, 1))
    return jnp.where(lane == last, 0.0, pltpu.roll(x, last, 1))


def chosen(n_space, low, packed, high, i, where):
    s = lax.axis_index("space")
    rows = packed.shape[0]
    if i < 2:
        return jnp.where(s > 0, low[i, where], 0.0)
    if i < rows + 2:
        return packed[i - 2, where]
    return jnp.where(s < n_space - 1, high[i - rows - 2, where], 0.0)


def forecast(n_space, low, packed, high, onehot, members):
    rows, _, cols = packed.shape
    sites = onehot.shape[1]

    def body(low, packed, high, hot, first, state, observed, tanh, sums):
        def row(i):
            return chosen(n_space, low, packed, high, i, slice(0, members))

        def aux(i, k):
            return chosen(n_space, low, packed, high, i, slice(members + k, members + k + 1))

        def step(center, north, south, i):
            return aux(i, 4) * (
                center
                + aux(i, 0) * (north - center)
                + aux(i, 1) * (south - center)
                + aux(i, 2) * (side(center, 1) - center)
                + aux(i, 3) * (side(center, -1) - center)
            )

        for i in range(1, rows + 3):
            first[i - 1] = step(row(i), row(i - 1), row(i + 1), i)
        picked = jnp.zeros((members, sites), jnp.float32)
        sums[...] = jnp.zeros_like(sums)
        for r in range(rows):
            state[r] = step(first[r + 1], first[r], first[r + 2], r + 2)
            sums[0, r : r + 1] = jnp.sum(state[r], axis=0, keepdims=True)
            picked = picked + lax.dot_general(
                state[r], hot[r], (((1,), (1,)), ((), ())), precision=HIGHEST,
                preferred_element_type=jnp.float32,
            )
        tanh[...] = jnp.tanh(picked)
        observed[...] = picked + 0.5 * tanh[...]

    shape = lambda *dims: jax.ShapeDtypeStruct(dims, jnp.float32)
    return pl.pallas_call(
        body,
        out_shape=(
            shape(rows + 2, members, cols), shape(rows, members, cols), shape(members, sites),
            shape(members, sites), shape(1, rows + -rows % 8, cols),
        ),
        in_specs=[VMEM_SPEC] * 4,
        out_specs=(VMEM_SPEC,) * 5,
        name="forecast",
    )(low, packed, high, onehot)


def prepare(n_mem, state, obs_full, sums, precision, data, cot_full):
    rows, members, cols = state.shape
    total, sites = obs_full.shape
    assert n_mem == 4
    middle = members // 2

    def nt3(a, b):
        plain = lambda x, y: lax.dot_general(
            x, y, (((1,), (1,)), ((), ())), preferred_element_type=jnp.float32
        )
        return plain(a[0], b[0]) + (plain(a[0], b[1]) + plain(a[1], b[0]))

    def body(state, obs, sums, prec, data, cot, block, anom, innov):
        m = lax.axis_index("mem")
        scale = jnp.sqrt(jnp.float32(total - 1))
        average = jnp.sum(sums[...], axis=0) / total
        mean = jnp.sum(obs[...], axis=0, keepdims=True) / total
        anom[...] = (obs[...] - mean) * prec[...] / scale
        innov[...] = prec[...] * (data[...] - mean)
        cross = jnp.zeros((members, total), jnp.float32)
        for r in range(rows):
            deviation = (state[r] - average[r : r + 1]) / scale
            cross = cross + nt3(split(deviation), split(cot[r]))
        block[:, :total] = cross
        at = lambda start, size: anom[pl.ds(pl.multiple_of(start, middle), size), :]
        own = at(m * members, members)
        own_split = split(own)
        block[:, total : total + members] = nt3(own_split, own_split)
        beside = at(lax.rem(m + 1, n_mem) * members, members)
        block[:, total + members : total + 2 * members] = nt3(own_split, split(beside))
        low, high = lax.rem(m, 2), m // 2
        halves = nt3(
            split(at(low * members, members)),
            split(at((low + 2) * members + high * middle, middle)),
        )
        pull = jnp.sum(own * innov[...], axis=1, keepdims=True)
        block[:, total + 2 * members :] = jnp.concatenate(
            [halves, jnp.broadcast_to(pull, (members, middle))], axis=1
        )

    shape = lambda *dims: jax.ShapeDtypeStruct(dims, jnp.float32)
    return pl.pallas_call(
        body,
        out_shape=(shape(members, total + 3 * members), shape(total, sites), shape(1, sites)),
        in_specs=[VMEM_SPEC] * 6,
        out_specs=(VMEM_SPEC,) * 3,
        name="prepare",
    )(state, obs_full, sums, precision, data, cot_full)


def backward(n_space, low_bar, second_bar, high_bar, low, packed, high, first_ext):
    rows, members, cols = second_bar.shape

    def body(low_bar, second, high_bar, low, packed, high, first_ext, grad, coef, first_bar):
        def bar(i):
            return chosen(n_space, low_bar, second, high_bar, i, slice(0, members))

        def prior(i):
            return chosen(n_space, low, packed, high, i, slice(0, members))

        def aux(i, k):
            return chosen(n_space, low, packed, high, i, slice(members + k, members + k + 1))

        def adjoint(center, north, south, i):
            keeping = 1.0 - aux(i, 0) - aux(i, 1) - aux(i, 2) - aux(i, 3)
            return (
                center * keeping
                + aux(i + 1, 0) * south
                + aux(i - 1, 1) * north
                + side(aux(i, 2) * center, -1)
                + side(aux(i, 3) * center, 1)
            )

        for i in range(1, rows + 3):
            first_bar[i - 1] = aux(i, 4) * adjoint(bar(i), bar(i - 1), bar(i + 1), i)
        for r in range(rows):
            grad[r] = adjoint(first_bar[r + 1], first_bar[r], first_bar[r + 2], r + 2)
            w2, c2 = second[r], first_ext[r + 1]
            w1, c1 = first_bar[r + 1], prior(r + 2)
            sides2 = (first_ext[r], first_ext[r + 2], side(c2, 1), side(c2, -1))
            sides1 = (prior(r + 1), prior(r + 3), side(c1, 1), side(c1, -1))
            for k in range(4):
                term = w2 * (sides2[k] - c2) + w1 * (sides1[k] - c1)
                coef[0, k * rows + r : k * rows + r + 1] = jnp.sum(term, axis=0, keepdims=True)

    shape = lambda *dims: jax.ShapeDtypeStruct(dims, jnp.float32)
    return pl.pallas_call(
        body,
        out_shape=(shape(rows, members, cols), shape(1, 4 * rows, cols)),
        in_specs=[VMEM_SPEC] * 7,
        out_specs=(VMEM_SPEC,) * 2,
        scratch_shapes=[pltpu.VMEM((rows + 2, members, cols), jnp.float32)],
        name="backward",
    )(low_bar, second_bar, high_bar, low, packed, high, first_ext)


def local(n_space, n_mem, prior, stencil, sea_mask, sites, data, precision, cotangent):
    members, rows, cols = prior.shape
    total = members * n_mem
    prior_t = jnp.transpose(prior, (1, 0, 2))
    cot_t = jnp.transpose(cotangent, (1, 0, 2))
    sea = sea_mask.astype(jnp.float32)[:, None]
    aux = jnp.concatenate(
        [jnp.transpose(stencil, (1, 0, 2)), sea, jnp.zeros((rows, 3, cols), jnp.float32)], axis=1
    )
    packed = jnp.concatenate([prior_t, aux], axis=1)
    low, high, cot_full = halo_gather(n_space, n_mem, packed[-2:], packed[:2], cot_t, 1)
    cells = jnp.arange(rows * cols, dtype=jnp.int32).reshape(rows, 1, cols)
    onehot = (sites[0][None, :, None] == cells).astype(jnp.float32)
    first_ext, state, observed, tanh_picked, sums = forecast(
        n_space, low, packed, high, onehot, members
    )
    obs_full, all_sums = gather_members(n_mem, [observed, sums], [0, 0], 3)
    block, anom_full, innovation = prepare(
        n_mem, state, obs_full, all_sums, precision[None], data[None], cot_full
    )
    block = block.reshape(n_space, members // n_space, -1)
    done = reduce_gather(n_space, n_mem, block, 4).reshape(total, -1)
    second_bar = analyse(
        done, cot_full, anom_full, innovation, precision[None], tanh_picked, onehot, sea, members
    )
    low_bar, high_bar = halo(n_space, second_bar[-2:], second_bar[:2], 5)
    prior_grad, coef_part = backward(
        n_space, low_bar, second_bar, high_bar, low, packed, high, first_ext
    )
    (coef_all,) = gather_members(n_mem, [coef_part], [0], 6)
    coef_total = jnp.sum(coef_all, axis=0).reshape(4, rows, cols)
    return (
        jnp.transpose(prior_grad, (1, 0, 2)),
        coef_total / jnp.sqrt(jnp.float32(total)),
    )


def solution(mesh):
    placed = (
        P("mem", "space", None),
        P(None, "space", None),
        P("space", None),
        P("space", None),
        P("space"),
        P("space"),
        P("mem", "space", None),
    )
    return jax.shard_map(
        functools.partial(local, mesh.shape["space"], mesh.shape["mem"]),
        mesh=mesh,
        in_specs=placed,
        out_specs=(P("mem", "space", None), P(None, "space", None)),
        check_vma=False,
    )
```

```python
import functools
import jax
import jax.numpy as jnp
from jax import lax
from jax.experimental import pallas as pl
from jax.experimental.pallas import tpu as pltpu
from jax.sharding import PartitionSpec as P

MESH = pl.DeviceIdType.MESH
HIGH = lax.Precision.HIGH
HIGHEST = lax.Precision.HIGHEST
VMEM_SPEC = pl.BlockSpec(memory_space=pltpu.VMEM)


def dot(a, b, a_dims, b_dims, precision=HIGH):
    return lax.dot_general(
        a, b, ((a_dims, b_dims), ((), ())), precision=precision, preferred_element_type=jnp.float32
    )


def mm(a, b):
    return dot(a, b, (1,), (0,))


def remote(src, dst, send, recv, s, m):
    return pltpu.make_async_remote_copy(
        src_ref=src, dst_ref=dst, send_sem=send, recv_sem=recv, device_id=(s, m), device_id_type=MESH
    )


def params(ident):
    return pltpu.CompilerParams(collective_id=ident, has_side_effects=True)


def halo_body(n_space, last, first, low, high, send, recv, others):
    s, m = lax.axis_index("space"), lax.axis_index("mem")
    barrier = pltpu.get_barrier_semaphore()
    has_low, has_high = s > 0, s < n_space - 1

    @pl.when(jnp.logical_not(has_low))
    def _():
        low[...] = jnp.zeros_like(low)

    @pl.when(jnp.logical_not(has_high))
    def _():
        high[...] = jnp.zeros_like(high)

    @pl.when(has_low)
    def _():
        pl.semaphore_signal(barrier, inc=1, device_id=(s - 1, m), device_id_type=MESH)

    @pl.when(has_high)
    def _():
        pl.semaphore_signal(barrier, inc=1, device_id=(s + 1, m), device_id_type=MESH)

    for peer in others:
        pl.semaphore_signal(barrier, inc=1, device_id=peer, device_id_type=MESH)
    pl.semaphore_wait(
        barrier, has_low.astype(jnp.int32) + has_high.astype(jnp.int32) + len(others)
    )

    up = remote(last, low, send.at[0], recv.at[0], s + 1, m)
    down = remote(first, high, send.at[1], recv.at[1], s - 1, m)

    @pl.when(has_high)
    def _():
        up.start()

    @pl.when(has_low)
    def _():
        down.start()

    def finish():
        @pl.when(has_low)
        def _():
            up.wait_recv()
            down.wait_send()

        @pl.when(has_high)
        def _():
            down.wait_recv()
            up.wait_send()

    return finish


def reduce_gather(n_space, n_mem, rows, ident):
    pieces, height, width = rows.shape
    near = 2 if n_space % 2 == 0 else 1
    far = n_space // near
    half = 2 if n_mem % 2 == 0 else 1
    wide = n_mem // half
    group = max(1, far // 4)
    groups = far // group

    def body(x, out, buf, rs_send, rs_recv, own, a_send, a_recv, b_send, b_recv, p_send, p_recv, q_send, q_recv):
        s, m = lax.axis_index("space"), lax.axis_index("mem")
        a, b = s // near, lax.rem(s, near)
        p, q = m // half, lax.rem(m, half)
        barrier = pltpu.get_barrier_semaphore()
        peers = [(lax.rem(s + k, n_space), m) for k in range(1, n_space)]
        peers += [(s, lax.rem(p + k, wide) * half + q) for k in range(1, wide)]
        peers += [(s, p * half + lax.rem(q + k, half)) for k in range(1, half)]
        for peer in peers:
            pl.semaphore_signal(barrier, inc=1, device_id=peer, device_id_type=MESH)
        mine = pltpu.make_async_copy(x.at[s], buf.at[s], own.at[0])
        mine.start()
        pl.semaphore_wait(barrier, len(peers))
        scatter = []
        for k in range(1, n_space):
            to = lax.rem(s + k, n_space)
            copy = remote(x.at[to], buf.at[s], rs_send.at[k], rs_recv.at[k], to, m)
            copy.start()
            scatter.append(copy)
        mine.wait()
        for copy in scatter:
            copy.wait_recv()
        total = buf[0]
        for k in range(1, n_space):
            total = total + buf[k]
        out[m, a, b] = total

        waits = list(scatter)
        stage_a = []
        for k in range(1, far):
            to = lax.rem(a + k, far)
            copy = remote(
                out.at[m, a, b], out.at[m, a, b], a_send.at[k], a_recv.at[k], to * near + b, m
            )
            copy.start()
            stage_a.append(copy)
        if group == 1:
            a_steps = [([], a)] + [([stage_a[k - 1]], lax.rem(a + far - k, far)) for k in range(1, far)]
        else:
            a_steps = [(stage_a if g == 0 else [], g * group) for g in range(groups)]
        steps_b = []
        for index, (needs, start) in enumerate(a_steps):
            for copy in needs:
                copy.wait_recv()
            steps_b.append((start, index))
            flow(
                out, s, m, b, p, q, start, index, 0, group, near, half, wide,
                b_send, b_recv, p_send, p_recv, q_send, q_recv, waits,
            )
        waits += stage_a
        for start, index in steps_b:
            pend = []
            for kb in range(1, near):
                pend.append((start, index, kb))
            for start_, index_, kb in pend:
                from_b = lax.rem(b + near - kb, near)
                piece = out.at[m, pl.ds(start_, group), from_b]
                remote(piece, piece, b_send.at[kb, index_], b_recv.at[kb, index_], s, m).wait_recv()
                flow(
                    out, s, m, from_b, p, q, start_, index_, kb, group, near, half, wide,
                    None, None, p_send, p_recv, q_send, q_recv, waits,
                )
        for start, index in steps_b:
            for kb in range(near):
                which_b = lax.rem(b + near - kb, near)
                for kp in range(1, wide):
                    from_p = lax.rem(p + wide - kp, wide)
                    piece = out.at[from_p * half + q, pl.ds(start, group), which_b]
                    remote(
                        piece, piece, p_send.at[kp, kb, index], p_recv.at[kp, kb, index], s, m
                    ).wait_recv()
                    for kq in range(1, half):
                        to_q = lax.rem(q + kq, half)
                        copy = remote(
                            piece, piece, q_send.at[kq, kp, kb, index], q_recv.at[kq, kp, kb, index],
                            s, p * half + to_q,
                        )
                        copy.start()
                        waits.append(copy)
        for start, index in steps_b:
            for kb in range(near):
                which_b = lax.rem(b + near - kb, near)
                for kp in range(wide):
                    from_p = lax.rem(p + wide - kp, wide)
                    for kq in range(1, half):
                        from_q = lax.rem(q + half - kq, half)
                        piece = out.at[from_p * half + from_q, pl.ds(start, group), which_b]
                        remote(
                            piece, piece, q_send.at[kq, kp, kb, index],
                            q_recv.at[kq, kp, kb, index], s, m,
                        ).wait_recv()
        for copy in waits:
            copy.wait_send()

    def flow(
        out, s, m, which_b, p, q, start, index, kb, group, near, half, wide,
        b_send, b_recv, p_send, p_recv, q_send, q_recv, waits,
    ):
        piece = out.at[m, pl.ds(start, group), which_b]
        for kp in range(1, wide):
            copy = remote(
                piece, piece, p_send.at[kp, kb, index], p_recv.at[kp, kb, index],
                s, lax.rem(p + kp, wide) * half + q,
            )
            copy.start()
            waits.append(copy)
        if b_send is not None:
            for k in range(1, near):
                to = (s // near) * near + lax.rem(which_b + k, near)
                copy = remote(piece, piece, b_send.at[k, index], b_recv.at[k, index], to, m)
                copy.start()
                waits.append(copy)
        for kq in range(1, half):
            copy = remote(
                piece, piece, q_send.at[kq, 0, kb, index], q_recv.at[kq, 0, kb, index],
                s, p * half + lax.rem(q + kq, half),
            )
            copy.start()
            waits.append(copy)

    dma = pltpu.SemaphoreType.DMA
    out = pl.pallas_call(
        body,
        out_shape=jax.ShapeDtypeStruct((n_mem, far, near, height, width), rows.dtype),
        in_specs=[VMEM_SPEC],
        out_specs=VMEM_SPEC,
        scratch_shapes=[
            pltpu.VMEM(rows.shape, rows.dtype),
            dma((n_space,)), dma((n_space,)), dma((1,)),
            dma((far,)), dma((far,)),
            dma((near, groups)), dma((near, groups)),
            dma((wide, near, groups)), dma((wide, near, groups)),
            dma((half, wide, near, groups)), dma((half, wide, near, groups)),
        ],
        compiler_params=params(ident),
        name="reduce_gather",
    )(rows)
    return out


def split(x):
    lead = x.astype(jnp.bfloat16)
    return lead, (x - lead.astype(jnp.float32)).astype(jnp.bfloat16)


def mm3(a, b):
    plain = lambda x, y: jnp.dot(x, y, preferred_element_type=jnp.float32)
    return plain(a[0], b[0]) + (plain(a[0], b[1]) + plain(a[1], b[0]))


def analyse(done, cot_full, anom_full, innovation, precision, tanh_picked, onehot, sea, members):
    total = done.shape[0]
    rows, _, cols = cot_full.shape

    def body(done, cot, anom, innov, prec, tanh, hot, sea, out, f_ref, f2_ref, t_ref, s_ref, u_ref, y_ref, v_ref):
        scale = jnp.sqrt(jnp.float32(total - 1))
        offset = pl.multiple_of(lax.axis_index("mem") * members, members)
        mine = pl.ds(offset, members)
        diagonal = lax.broadcasted_iota(jnp.int32, (total, total), 0) == lax.broadcasted_iota(
            jnp.int32, (total, total), 1
        )
        identity = diagonal.astype(jnp.float32)
        whole = lambda x: jnp.sum(jnp.sum(x, axis=0, keepdims=True), axis=1, keepdims=True)
        for p in range(4):
            here, there = pl.ds(p * members, members), pl.ds((p + 1) % 4 * members, members)
            s_ref[here, here] = done[here, total : total + members]
            edge = done[here, total + members : total + 2 * members]
            s_ref[here, there] = edge
            s_ref[there, here] = edge.T
        for p in range(2):
            here, there = pl.ds(p * members, members), pl.ds((p + 2) * members, members)
            pair = slice(total + 2 * members, total + 2 * members + members // 2)
            edge = jnp.concatenate([done[here, pair], done[there, pair]], axis=1)
            s_ref[here, there] = edge
            s_ref[there, here] = edge.T
        system = identity + s_ref[...]
        norm = jnp.sqrt(whole(system * system))
        root = jnp.sqrt(norm)
        f_ref[...] = 1.5 * identity - 0.5 * (system / norm)
        f_split = split(f_ref[...])
        f2_ref[...] = mm3(f_split, f_split)
        f2_split = split(f2_ref[...])
        t_ref[...] = (
            1.5 * f_ref[...] + mm3(f2_split, split(f2_ref[...] - 1.5 * f_ref[...]))
        ) / root
        t_split = split(t_ref[...])
        pull = jnp.broadcast_to(done[:, total + 3 * members - 1 :], (total, 128))
        mean_bar = jnp.sum(done[:, :total], axis=1, keepdims=True)
        first = mm3(t_split, split(jnp.concatenate([pull, jnp.broadcast_to(mean_bar, pull.shape)], axis=1)))
        v_ref[...] = mm3(t_split, split(first))
        width = pull.shape[1]
        row = lambda x: x.T[:1]
        s_ref[...] = (
            scale * done[:, :total]
            + mean_bar * row(first[:, :width])
            + first[:, width : width + 1] * row(pull)
        )
        weight = 0.5 * (s_ref[...] + s_ref[...].T)
        scale_bar = -0.5 * whole(weight * t_ref[...]) / norm
        s_ref[...] = weight / root
        s_split = split(s_ref[...])
        u_ref[...] = mm3(s_split, f2_split)
        y_ref[...] = mm3(s_split, split(2.0 * f2_ref[...] - 1.5 * f_ref[...]))
        y_ref[...] = 0.5 * (y_ref[...] + y_ref[...].T)
        approach = 1.5 * s_ref[...] - 1.5 * u_ref[...]
        approach = whole(
            approach * (3.0 * identity - 2.0 * f_ref[...])
            + 2.0 * y_ref[...] * (3.0 * f_ref[...] - 2.0 * f2_ref[...])
        )
        scale_bar = scale_bar + 0.5 * approach / norm

        centred = lambda ref: ref[mine, :] - jnp.sum(ref[...], axis=0, keepdims=True) / total
        f_mine = centred(f_ref)
        bar = 1.5 * centred(s_ref) - 0.75 * (centred(u_ref) + mm3(split(centred(f2_ref)), s_split))
        bar = bar + mm3(split(centred(y_ref)), f_split) + mm3(split(f_mine), split(y_ref[...]))
        unit = (
            lax.broadcasted_iota(jnp.int32, (members, total), 0) + offset
            == lax.broadcasted_iota(jnp.int32, (members, total), 1)
        ).astype(jnp.float32) - 1.0 / total
        system_mine = norm * (3.0 * unit - 2.0 * f_mine)
        sym = 2.0 * (-0.5 * bar + scale_bar * system_mine) / norm
        pull_bar = v_ref[:, width:]
        sym = sym - (scale / total) * row(pull_bar)
        pull_mine = v_ref[mine, width:][:, :1] - jnp.sum(pull_bar[:, :1], axis=0, keepdims=True) / total
        mean_weights = v_ref[:, :1]
        mix = t_ref[mine, :] + v_ref[mine, :width][:, :1] / scale
        row_weights = (
            jnp.sum(t_ref[...], axis=0, keepdims=True)
            + jnp.sum(mean_weights, axis=0, keepdims=True) / scale
        )
        mix = mix + (1.0 - row_weights) / total
        observed = (prec[...] / scale) * (mm3(split(sym), split(anom[...])) + pull_mine * innov[...])
        picked = observed * (1.0 + 0.5 * (1.0 - tanh[...] * tanh[...]))
        mix_split, picked_split = split(mix), split(picked)
        for r in range(rows):
            mark = hot[r].astype(jnp.bfloat16)
            spread = jnp.dot(picked_split[0], mark, preferred_element_type=jnp.float32) + jnp.dot(
                picked_split[1], mark, preferred_element_type=jnp.float32
            )
            out[r] = sea[r] * (mm3(mix_split, split(cot[r])) + spread)

    square = pltpu.VMEM((total, total), jnp.float32)
    return pl.pallas_call(
        body,
        out_shape=jax.ShapeDtypeStruct((rows, members, cols), jnp.float32),
        in_specs=[VMEM_SPEC] * 8,
        out_specs=VMEM_SPEC,
        scratch_shapes=[square] * 6 + [pltpu.VMEM((total, 256), jnp.float32)],
        compiler_params=pltpu.CompilerParams(vmem_limit_bytes=60 * 1024 * 1024),
        cost_estimate=pl.CostEstimate(flops=10 * total**3, bytes_accessed=8 * total**2, transcendentals=0),
        name="analyse",
    )(done, cot_full, anom_full, innovation, precision, tanh_picked, onehot, sea)


def side(x, step):
    lane = lax.broadcasted_iota(jnp.int32, x.shape, 1)
    last = x.shape[1] - 1
    if step > 0:
        return jnp.where(lane == 0, 0.0, pltpu.roll(x, 1, 1))
    return jnp.where(lane == last, 0.0, pltpu.roll(x, last, 1))


def chosen(n_space, low, packed, high, i, where):
    s = lax.axis_index("space")
    rows = packed.shape[0]
    if i < 2:
        return jnp.where(s > 0, low[i, where], 0.0)
    if i < rows + 2:
        return packed[i - 2, where]
    return jnp.where(s < n_space - 1, high[i - rows - 2, where], 0.0)


def member_sends(n_mem, piece, send, recv):
    s, m = lax.axis_index("space"), lax.axis_index("mem")
    copies = []
    for k in range(1, n_mem):
        copies.append(remote(piece, piece, send.at[k], recv.at[k], s, lax.rem(m + k, n_mem)))
        copies[-1].start()
    return copies


def forecast(n_space, n_mem, packed, block, onehot, members, ident):
    rows, depth, cols = packed.shape
    sites = onehot.shape[1]
    half = 2 if n_mem % 2 == 0 else 1
    wide = n_mem // half

    def body(
        packed, x, hot, low, high, out, first, state, observed, tanh, sums,
        send, recv, own, p_send, p_recv, q_send, q_recv, o_send, o_recv, t_send, t_recv,
    ):
        s, m = lax.axis_index("space"), lax.axis_index("mem")
        p, q = m // half, lax.rem(m, half)
        across = [lax.rem(p + k, wide) * half + q for k in range(1, wide)]
        beside = [p * half + lax.rem(q + k, half) for k in range(1, half)]

        def part(which):
            return out.at[:, pl.ds(pl.multiple_of(which * members, members), members)]

        mine = pltpu.make_async_copy(x, part(m), own.at[0])
        mine.start()
        finish = halo_body(
            n_space, packed.at[pl.ds(rows - 2, 2)], packed.at[pl.ds(0, 2)], low, high, send, recv,
            [(s, lax.rem(m + k, n_mem)) for k in range(1, n_mem)],
        )
        copies = []
        for k, to in enumerate(across):
            copies.append(remote(x, part(m), p_send.at[k], p_recv.at[k], s, to))
            copies[-1].start()
        hops = list(copies)
        for k, to in enumerate(beside):
            copies.append(remote(x, part(m), q_send.at[k, 0], q_recv.at[k, 0], s, to))
            copies[-1].start()
        finish()
        for kp, hop in enumerate(hops):
            from_p = lax.rem(p + wide - kp - 1, wide)
            hop.wait_recv()
            piece = part(from_p * half + q)
            for k, to in enumerate(beside):
                copies.append(remote(piece, piece, q_send.at[k, kp + 1], q_recv.at[k, kp + 1], s, to))
                copies[-1].start()

        def row(i):
            return chosen(n_space, low, packed, high, i, slice(0, members))

        def aux(i, k):
            return chosen(n_space, low, packed, high, i, slice(members + k, members + k + 1))

        def step(center, north, south, i):
            return aux(i, 4) * (
                center
                + aux(i, 0) * (north - center)
                + aux(i, 1) * (south - center)
                + aux(i, 2) * (side(center, 1) - center)
                + aux(i, 3) * (side(center, -1) - center)
            )

        for i in range(1, rows + 3):
            first[i - 1] = step(row(i), row(i - 1), row(i + 1), i)
        picked = jnp.zeros((members, sites), jnp.float32)
        lines = []
        for r in range(rows):
            state[r] = step(first[r + 1], first[r], first[r + 2], r + 2)
            lines.append(jnp.sum(state[r], axis=0, keepdims=True))
            picked = picked + lax.dot_general(
                state[r], hot[r], (((1,), (1,)), ((), ())), precision=HIGHEST,
                preferred_element_type=jnp.float32,
            )
        lines.append(jnp.zeros((-rows % 8, cols), jnp.float32))
        sums[m] = jnp.concatenate(lines, axis=0)
        tanh[...] = jnp.tanh(picked)
        slot = pl.ds(pl.multiple_of(m * members, members), members)
        observed[slot, :] = picked + 0.5 * tanh[...]
        last = member_sends(n_mem, observed.at[slot], o_send, o_recv)
        last += member_sends(n_mem, sums.at[m], t_send, t_recv)
        mine.wait()
        for copy in copies[len(hops) :] + last:
            copy.wait_recv()
        for copy in copies + last:
            copy.wait_send()

    shape = lambda *dims: jax.ShapeDtypeStruct(dims, jnp.float32)
    dma = pltpu.SemaphoreType.DMA
    return pl.pallas_call(
        body,
        out_shape=(
            shape(2, depth, cols), shape(2, depth, cols), shape(rows, n_mem * members, cols),
            shape(rows + 2, members, cols), shape(rows, members, cols),
            shape(n_mem * members, sites), shape(members, sites),
            shape(n_mem, rows + -rows % 8, cols),
        ),
        in_specs=[VMEM_SPEC] * 3,
        out_specs=(VMEM_SPEC,) * 8,
        scratch_shapes=[
            dma((2,)), dma((2,)), dma((1,)), dma((wide,)), dma((wide,)),
            dma((half, wide)), dma((half, wide)),
            dma((n_mem,)), dma((n_mem,)), dma((n_mem,)), dma((n_mem,)),
        ],
        compiler_params=params(ident),
        name="forecast",
    )(packed, block, onehot)


def prepare(n_mem, state, obs_full, sums, precision, data, cot_full):
    rows, members, cols = state.shape
    total, sites = obs_full.shape
    assert n_mem == 4
    middle = members // 2

    def nt3(a, b):
        plain = lambda x, y: lax.dot_general(
            x, y, (((1,), (1,)), ((), ())), preferred_element_type=jnp.float32
        )
        return plain(a[0], b[0]) + (plain(a[0], b[1]) + plain(a[1], b[0]))

    def body(state, obs, sums, prec, data, cot, block, anom, innov):
        m = lax.axis_index("mem")
        scale = jnp.sqrt(jnp.float32(total - 1))
        average = jnp.sum(sums[...], axis=0) / total
        mean = jnp.sum(obs[...], axis=0, keepdims=True) / total
        anom[...] = (obs[...] - mean) * prec[...] / scale
        innov[...] = prec[...] * (data[...] - mean)
        cross = jnp.zeros((members, total), jnp.float32)
        for r in range(rows):
            deviation = (state[r] - average[r : r + 1]) / scale
            cross = cross + nt3(split(deviation), split(cot[r]))
        block[:, :total] = cross
        at = lambda start, size: anom[pl.ds(pl.multiple_of(start, middle), size), :]
        own = at(m * members, members)
        own_split = split(own)
        block[:, total : total + members] = nt3(own_split, own_split)
        beside = at(lax.rem(m + 1, n_mem) * members, members)
        block[:, total + members : total + 2 * members] = nt3(own_split, split(beside))
        low, high = lax.rem(m, 2), m // 2
        halves = nt3(
            split(at(low * members, members)),
            split(at((low + 2) * members + high * middle, middle)),
        )
        pull = jnp.sum(own * innov[...], axis=1, keepdims=True)
        block[:, total + 2 * members :] = jnp.concatenate(
            [halves, jnp.broadcast_to(pull, (members, middle))], axis=1
        )

    shape = lambda *dims: jax.ShapeDtypeStruct(dims, jnp.float32)
    return pl.pallas_call(
        body,
        out_shape=(shape(members, total + 3 * members), shape(total, sites), shape(1, sites)),
        in_specs=[VMEM_SPEC] * 6,
        out_specs=(VMEM_SPEC,) * 3,
        name="prepare",
    )(state, obs_full, sums, precision, data, cot_full)


def backward(n_space, n_mem, second_bar, low, packed, high, first_ext, ident):
    rows, members, cols = second_bar.shape

    def body(
        second, low, packed, high, first_ext, grad, coef, low_bar, high_bar, first_bar,
        send, recv, c_send, c_recv,
    ):
        s, m = lax.axis_index("space"), lax.axis_index("mem")
        halo_body(
            n_space, second.at[pl.ds(rows - 2, 2)], second.at[pl.ds(0, 2)], low_bar, high_bar,
            send, recv, [(s, lax.rem(m + k, n_mem)) for k in range(1, n_mem)],
        )()

        def bar(i):
            return chosen(n_space, low_bar, second, high_bar, i, slice(0, members))

        def prior(i):
            return chosen(n_space, low, packed, high, i, slice(0, members))

        def aux(i, k):
            return chosen(n_space, low, packed, high, i, slice(members + k, members + k + 1))

        def adjoint(center, north, south, i):
            keeping = 1.0 - aux(i, 0) - aux(i, 1) - aux(i, 2) - aux(i, 3)
            return (
                center * keeping
                + aux(i + 1, 0) * south
                + aux(i - 1, 1) * north
                + side(aux(i, 2) * center, -1)
                + side(aux(i, 3) * center, 1)
            )

        for i in range(1, rows + 3):
            first_bar[i - 1] = aux(i, 4) * adjoint(bar(i), bar(i - 1), bar(i + 1), i)
        lines = [[None] * rows for _ in range(4)]
        for r in range(rows):
            w2, c2 = second[r], first_ext[r + 1]
            w1, c1 = first_bar[r + 1], prior(r + 2)
            sides2 = (first_ext[r], first_ext[r + 2], side(c2, 1), side(c2, -1))
            sides1 = (prior(r + 1), prior(r + 3), side(c1, 1), side(c1, -1))
            for k in range(4):
                term = w2 * (sides2[k] - c2) + w1 * (sides1[k] - c1)
                lines[k][r] = jnp.sum(term, axis=0, keepdims=True)
        coef[m] = jnp.concatenate([line for group in lines for line in group], axis=0)
        copies = member_sends(n_mem, coef.at[m], c_send, c_recv)
        for r in range(rows):
            grad[r] = adjoint(first_bar[r + 1], first_bar[r], first_bar[r + 2], r + 2)
        for copy in copies:
            copy.wait()

    shape = lambda *dims: jax.ShapeDtypeStruct(dims, jnp.float32)
    edge = pltpu.VMEM((2, members, cols), jnp.float32)
    dma = pltpu.SemaphoreType.DMA
    return pl.pallas_call(
        body,
        out_shape=(shape(rows, members, cols), shape(n_mem, 4 * rows, cols)),
        in_specs=[VMEM_SPEC] * 5,
        out_specs=(VMEM_SPEC,) * 2,
        scratch_shapes=[
            edge, edge, pltpu.VMEM((rows + 2, members, cols), jnp.float32),
            dma((2,)), dma((2,)), dma((n_mem,)), dma((n_mem,)),
        ],
        compiler_params=params(ident),
        name="backward",
    )(second_bar, low, packed, high, first_ext)


def local(n_space, n_mem, prior, stencil, sea_mask, sites, data, precision, cotangent):
    members, rows, cols = prior.shape
    total = members * n_mem
    prior_t = jnp.transpose(prior, (1, 0, 2))
    cot_t = jnp.transpose(cotangent, (1, 0, 2))
    sea = sea_mask.astype(jnp.float32)[:, None]
    aux = jnp.concatenate(
        [jnp.transpose(stencil, (1, 0, 2)), sea, jnp.zeros((rows, 3, cols), jnp.float32)], axis=1
    )
    packed = jnp.concatenate([prior_t, aux], axis=1)
    cells = jnp.arange(rows * cols, dtype=jnp.int32).reshape(rows, 1, cols)
    onehot = (sites[0][None, :, None] == cells).astype(jnp.float32)
    low, high, cot_full, first_ext, state, obs_full, tanh_picked, all_sums = forecast(
        n_space, n_mem, packed, cot_t, onehot, members, 1
    )
    block, anom_full, innovation = prepare(
        n_mem, state, obs_full, all_sums, precision[None], data[None], cot_full
    )
    block = block.reshape(n_space, members // n_space, -1)
    done = reduce_gather(n_space, n_mem, block, 3).reshape(total, -1)
    second_bar = analyse(
        done, cot_full, anom_full, innovation, precision[None], tanh_picked, onehot, sea, members
    )
    prior_grad, coef_all = backward(
        n_space, n_mem, second_bar, low, packed, high, first_ext, 2
    )
    coef_total = jnp.sum(coef_all, axis=0).reshape(4, rows, cols)
    return (
        jnp.transpose(prior_grad, (1, 0, 2)),
        coef_total / jnp.sqrt(jnp.float32(total)),
    )


def solution(mesh):
    placed = (
        P("mem", "space", None),
        P(None, "space", None),
        P("space", None),
        P("space", None),
        P("space"),
        P("space"),
        P("mem", "space", None),
    )
    return jax.shard_map(
        functools.partial(local, mesh.shape["space"], mesh.shape["mem"]),
        mesh=mesh,
        in_specs=placed,
        out_specs=(P("mem", "space", None), P(None, "space", None)),
        check_vma=False,
    )
```
